32 devices in a mesh: groups: 2 (over x), rows: 16 (over z, y, core).
Axes of the slice: x: 2, y: 2, z: 4, core: 2. Of those that a mesh axis runs over, the one named last changes fastest.
Arguments:
- features: bfloat16 [3, 256, 8192], P(None, ('groups', 'rows')), parts along dimension 1, may hold values from -6 to 6
- carried: bfloat16 [2, 256, 8192], P(None, ('groups', 'rows')), parts along dimension 1, may hold values from -6 to 6
- flow_shift: int32 [3, 32, 2], P(None, ('groups', 'rows')), parts along dimension 1, may hold values from -8 to 8, as said below
- clip_start: int32 [8], P('groups'), parts along dimension 0, may hold values from 0 to 3
- join_weight: bfloat16 [3, 576, 64], replicated, may hold values from -0.15625 to 0.15625
- res_weight: bfloat16 [4, 3, 192, 64], replicated, may hold values from -0.25 to 0.25
Outputs:
- propagated: bfloat16 [3, 256, 8192], P(None, ('groups', 'rows')), parts along dimension 1
The draws below stay inside these ranges and needn't reach their ends.
There are 2 independent parts, one for each index of `groups`. The reference program is written for one: setup_inputs(seed, part) draws one part's arguments, and reference() takes and returns one part's arrays. A program takes and returns all parts, laid end to end along the dimension named above; an argument that names none is the same for every part. Nothing has to cross between parts.
Inputs may be any that keep to these rules, and one draw needn't show every extreme that they name: `flow_shift`: both ends of the range occur in every draw. `clip_start`: 3 means that the owner begins no clip in these steps.
All inputs are finite; a program needn't handle non-finite values.
Results may differ from the reference program's by a relative error of at most 0.014.
Values may be sent and summed in bfloat16 or wider, within the bound.
No kernel may reach another device: no remote copies, remote signals or barrier semaphores. Data moves between devices by JAX's collectives and lax.ppermute only.
A program may use at most 64 MiB of HBM per device.

```python
import jax
import jax.numpy as jnp
from jax import lax

C = 64
BAND = 8
WIN = 128
TICKS = 3
SECTIONS = 4
RES_BLOCKS = 2
MAXSHIFT = 8
SLOTS = 16
ALLROWS = 128
WIDE = 8192


def draw_flow_shift(key, part):
    total = TICKS * SLOTS * 2
    base = jax.random.randint(jax.random.fold_in(key, 11), (total,), -MAXSHIFT, MAXSHIFT + 1).astype(jnp.int32)
    spot_one = jax.random.randint(jax.random.fold_in(key, 12), (), 0, total)
    spot_gap = jax.random.randint(jax.random.fold_in(key, 13), (), 1, total)
    spot_two = (spot_one + spot_gap) % total
    base = base.at[spot_one].set(MAXSHIFT)
    base = base.at[spot_two].set(-MAXSHIFT)
    return base.reshape(TICKS, SLOTS, 2).astype(jnp.int32)


def touch_ends(entries, key, low, top_value):
    longest = entries.shape.index(max(entries.shape))
    spots = []
    for shift in (0, 1):
        where = [jax.random.randint(jax.random.fold_in(key, axis), (), 0, length) for axis, length in enumerate(entries.shape)]
        where[longest] = (where[longest] + shift) % entries.shape[longest]
        spots.append(tuple(where))
    return entries.at[spots[0]].set(low).at[spots[1]].set(top_value)


def level_of(rng, dims, pieces, low, top_value):
    def one(dim, shards_of):
        steps = jax.random.uniform(jax.random.fold_in(jax.random.fold_in(rng, 6), dim), (shards_of,), jnp.float32, low / len(pieces), top_value / len(pieces))
        return jnp.repeat(jnp.exp(steps), dims[dim] // shards_of).reshape((-1,) + (1,) * (len(dims) - dim - 1))

    loudness = one(*pieces[0])
    for cut in pieces[1:]:
        loudness = loudness * one(*cut)
    return loudness


def gaussian(own_key, shape, width, most, split=(), held_as=jnp.bfloat16):
    drawn = jax.random.normal(own_key, shape, jnp.float32) * width
    if len(split) > 0:
        drawn = level_of(own_key, shape, split, -0.22, 0.18) * drawn
    return jnp.clip(drawn, min=-most, max=most).astype(held_as)


def setup_inputs(seed: int = 0, part: int = 0) -> dict:
    splits = jax.random.split(jax.random.key(seed), 7)
    part_splits = jax.random.split(jax.random.fold_in(splits[6], part), 7)
    features = gaussian(part_splits[0], (TICKS, ALLROWS, WIDE), 1.0, 6.0, ((1, 16),))
    carried = gaussian(part_splits[1], (2, ALLROWS, WIDE), 1.0, 6.0, ((1, 16),))
    flow_shift = draw_flow_shift(jax.random.fold_in(jax.random.fold_in(splits[6], part), 71), part)
    clip_start = touch_ends(jax.random.randint(part_splits[3], (SECTIONS,), 0, TICKS + 1), jax.random.fold_in(part_splits[3], 1), 0, TICKS).astype(jnp.int32)
    join_weight = gaussian(splits[4], (3, 9 * C, C), (27 * C) ** -0.5, 0.15625)
    res_weight = gaussian(splits[5], (2 * RES_BLOCKS, 3, 3 * C, C), (9 * C) ** -0.5, 0.25)
    return {"features": features, "carried": carried, "flow_shift": flow_shift, "clip_start": clip_start, "join_weight": join_weight, "res_weight": res_weight}


def leaky_relu(values):
    return jnp.where(values >= 0, values, 0.1 * values)


def frame_conv(frames, weight):
    count = frames.shape[0]
    height = frames.shape[1]
    column_count = frames.shape[2]
    padded = jnp.pad(frames, ((0, 0), (1, 1), (1, 1), (0, 0)))
    columns = jnp.concatenate([padded[:, :, 0:column_count], padded[:, :, 1:column_count + 1], padded[:, :, 2:column_count + 2]], axis=3)
    depth_in = columns.shape[3]
    summed = jnp.dot(columns[:, 0:height].reshape(-1, depth_in), weight[0], preferred_element_type=jnp.float32)
    summed = summed + jnp.dot(columns[:, 1:height + 1].reshape(-1, depth_in), weight[1], preferred_element_type=jnp.float32)
    summed = summed + jnp.dot(columns[:, 2:height + 2].reshape(-1, depth_in), weight[2], preferred_element_type=jnp.float32)
    return summed.reshape(count, height, column_count, weight.shape[2])


def realign(latest, offsets):
    padded = jnp.pad(latest, ((0, 0), (0, 0), (MAXSHIFT * C, MAXSHIFT * C)))

    def pick(piece, offset):
        return lax.dynamic_slice_in_dim(piece, ((MAXSHIFT - offset) * C).astype(jnp.int32), WIN * C, 1)

    return jax.vmap(pick)(padded, offsets.astype(jnp.int32))


def reference(features, carried, flow_shift, clip_start, join_weight, res_weight):
    slots = flow_shift.shape[1]
    per_owner = slots // SECTIONS
    offset_lead = per_owner // 2
    latest = jnp.roll(carried[0].reshape(slots, BAND, WIN * C), -offset_lead, axis=0)
    earlier = jnp.roll(carried[1].reshape(slots, BAND, WIN * C), -offset_lead, axis=0)
    shifts_all = jnp.roll(flow_shift, -offset_lead, axis=1)
    owner_of = (jnp.arange(slots) // per_owner).astype(jnp.int32)
    start_slot = clip_start[owner_of]
    results = []
    for frame_tick in range(TICKS):
        keep_state = (start_slot != frame_tick)[:, None, None]
        latest = jnp.where(keep_state, latest, jnp.zeros_like(latest))
        earlier = jnp.where(keep_state, earlier, jnp.zeros_like(earlier))
        warped_one = realign(latest, shifts_all[frame_tick, :, 0])
        warped_two = realign(earlier, shifts_all[frame_tick, :, 1])
        frame_feat = jnp.roll(features[frame_tick].reshape(slots, BAND, WIN * C), -offset_lead, axis=0)
        stacked = jnp.concatenate([warped_one.reshape(slots, BAND, WIN, C), warped_two.reshape(slots, BAND, WIN, C), frame_feat.reshape(slots, BAND, WIN, C)], axis=3)
        frames = stacked.reshape(SECTIONS, per_owner * BAND, WIN, 3 * C)
        current = leaky_relu(frame_conv(frames, join_weight)).astype(jnp.bfloat16)
        for res_index in range(RES_BLOCKS):
            middle = jnp.maximum(frame_conv(current, res_weight[2 * res_index]), 0.0).astype(jnp.bfloat16)
            current = (current.astype(jnp.float32) + frame_conv(middle, res_weight[2 * res_index + 1])).astype(jnp.bfloat16)
        flattened = current.reshape(slots, BAND, WIN * C)
        results.append(jnp.roll(flattened, offset_lead, axis=0).reshape(slots * BAND, WIN * C))
        latest, earlier = jnp.roll(flattened, per_owner, axis=0), jnp.roll(latest, per_owner, axis=0)
    return jnp.stack(results)
```

```python
import jax
import jax.numpy as jnp
from jax import lax
from jax.experimental import pallas as pl
from jax.experimental.pallas import tpu as pltpu
from jax.sharding import PartitionSpec as P

TICKS = 3
SECTIONS = 4
RES_BLOCKS = 2
MAXSHIFT = 8
RIM = 1 + 2 * RES_BLOCKS
PAD = 8

BF16 = jnp.bfloat16
F32 = jnp.float32
VMEM = pl.BlockSpec(memory_space=pltpu.VMEM)
SMEM = pl.BlockSpec(memory_space=pltpu.SMEM)


def neighbour_masks(pairs, lanes):
    lane = lax.broadcasted_iota(jnp.int32, (pairs, lanes), 1)
    pair = lax.broadcasted_iota(jnp.int32, (pairs, lanes), 0)
    half = lanes // 2
    return (lane < half) & (pair < pairs - 1), (lane >= half) & (pair > 0)


def put(dst, index, row, masks):
    pairs, lanes = row.shape
    after = pltpu.roll(row, pairs - 1, 0)
    before = pltpu.roll(row, 1, 0)
    beside = jnp.where(masks[0], after, jnp.where(masks[1], before, 0.0))
    dst[index + (slice(None), slice(0, lanes))] = row.astype(BF16)
    dst[index + (slice(None), slice(lanes, 2 * lanes))] = beside.astype(BF16)


def two_row_weight(w_ref, layer):
    zero = jnp.zeros(w_ref.shape[2:], BF16)
    w = [w_ref[layer, a] for a in range(3)]
    blocks = [[w[0], zero], [w[1], w[0]], [w[2], w[1]], [zero, w[2]]]
    return jnp.concatenate([jnp.concatenate(b, axis=1) for b in blocks], axis=0)


def two_row_conv(source, first, count, weight):
    columns = [
        jnp.concatenate([source[2 * (first + k) + i] for k in range(count)], axis=0)
        for i in range(4)
    ]
    return jnp.dot(
        jnp.concatenate(columns, axis=1), weight, preferred_element_type=F32
    )


def fetch_shift(padded, row, shift, odd_mask):
    pairs = padded.shape[1] - 2 * PAD
    lanes = padded.shape[2]
    whole = shift >> 1
    here = padded[row, pl.ds(PAD - whole, pairs), :]
    back = padded[row, pl.ds(PAD - 1 - whole, pairs), :]
    odd = pltpu.roll(jnp.where(odd_mask, back, here), lanes // 2, 1)
    return jnp.where((shift & 1) == 1, odd, here)


def odd_lanes(pairs, lanes):
    return lax.broadcasted_iota(jnp.int32, (pairs, lanes), 1) >= lanes // 2


def scalars_of(row):
    pairs = row.shape[0]
    wide = row.astype(F32)
    return (
        jnp.max(wide[0 : pairs // 2]).astype(jnp.int32),
        jnp.max(wide[pairs // 2 :]).astype(jnp.int32),
    )


def local_span(band_rows):
    return (RIM + 1) // 2, (RIM + band_rows - 4) // 2 + 1


def clear_pads(padded):
    rows, long, lanes = padded.shape
    padded[:, 0:PAD, :] = jnp.zeros((rows, PAD, lanes), F32)
    padded[:, long - PAD :, :] = jnp.zeros((rows, PAD, lanes), F32)


def start_kernel(info, own, w_ref, acc, ops, padded):
    parts, rows, pairs, lanes = own.shape
    masks = neighbour_masks(pairs, lanes)
    odd_mask = odd_lanes(pairs, lanes)
    clear_pads(padded)
    for part in range(2):

        def stage(r, _):
            row = own[part, r].astype(F32)
            padded[r, PAD : PAD + pairs, :] = jnp.where(info[3] == 1, row, 0.0)
            return 0

        lax.fori_loop(0, rows, stage, 0, unroll=2)
        shift = info[5 + part]

        def warp(r, _):
            put(ops, (part, r), fetch_shift(padded, r, shift, odd_mask), masks)
            return 0

        lax.fori_loop(0, rows, warp, 0, unroll=2)

    def plain(r, _):
        put(ops, (2, r), own[2, r].astype(F32), masks)
        return 0

    lax.fori_loop(0, rows, plain, 0, unroll=2)
    low, high = local_span(rows)
    total = None
    for part in range(3):
        columns = [
            jnp.concatenate(
                [ops[part, 2 * k + i - RIM] for k in range(low, high)], axis=0
            )
            for i in range(4)
        ]
        term = jnp.dot(
            jnp.concatenate(columns, axis=1),
            two_row_weight(w_ref, part),
            preferred_element_type=F32,
        )
        total = term if total is None else total + term
    acc[low * pairs : high * pairs] = total


def ahead_kernel(
    info, latest, prev, prev_one, prev_two, feat, feat_one, feat_two, w_ref,
    acc, ops, shifts, padded, window, first_step,
):
    rows, pairs, lanes = latest.shape
    masks = neighbour_masks(pairs, lanes)
    odd_mask = odd_lanes(pairs, lanes)
    even = info[0] == 1
    above_ok = info[1] == 1
    below_ok = info[2] == 1
    keep_latest = info[3] == 1
    keep_earlier = info[4] == 1
    own_shift = scalars_of(feat[0])
    above_shift = scalars_of(jnp.where(even, feat_two[RIM], feat_one[RIM]))
    below_shift = scalars_of(jnp.where(even, feat_one[0], feat_two[0]))
    shifts[0] = above_shift[0]
    shifts[1] = below_shift[0]
    clear_pads(padded)
    base = 1 if first_step else 0

    def prev_above(r):
        return jnp.where(even, prev_two[r], prev_one[r])

    def prev_below(r):
        return jnp.where(even, prev_one[base + r], prev_two[base + r])

    for first, count, source, ok, shift in (
        (0, RIM, prev_above, above_ok & keep_earlier, above_shift[1]),
        (RIM, rows, lambda r: prev[r], keep_earlier, own_shift[1]),
        (RIM + rows, RIM, prev_below, below_ok & keep_earlier, below_shift[1]),
    ):

        def stage(r, _):
            padded[first + r, PAD : PAD + pairs, :] = jnp.where(
                ok, source(r).astype(F32), 0.0
            )
            return 0

        lax.fori_loop(0, count, stage, 0)

        def warp(r, _):
            put(window, (0, first + r), fetch_shift(padded, first + r, shift, odd_mask), masks)
            return 0

        lax.fori_loop(0, count, warp, 0, unroll=2)

    for first, count, source, ok in (
        (0, RIM, lambda r: jnp.where(even, feat_two[r], feat_one[r]), above_ok),
        (RIM, rows, lambda r: feat[1 + r], None),
        (RIM + rows, RIM, lambda r: jnp.where(even, feat_one[1 + r], feat_two[1 + r]), below_ok),
    ):

        def plain(r, _):
            row = source(r).astype(F32)
            put(window, (1, first + r), row if ok is None else jnp.where(ok, row, 0.0), masks)
            return 0

        lax.fori_loop(0, count, plain, 0, unroll=2)

    count = (rows + 2 * RIM - 2) // 2
    acc[...] = two_row_conv(window.at[0], 0, count, two_row_weight(w_ref, 1))
    acc[...] += two_row_conv(window.at[1], 0, count, two_row_weight(w_ref, 2))

    def stage_latest(r, _):
        padded[r, PAD : PAD + pairs, :] = jnp.where(keep_latest, latest[r].astype(F32), 0.0)
        return 0

    lax.fori_loop(0, rows, stage_latest, 0, unroll=2)

    def warp_latest(r, _):
        put(ops, (0, r), fetch_shift(padded, r, own_shift[0], odd_mask), masks)
        return 0

    lax.fori_loop(0, rows, warp_latest, 0, unroll=2)
    low, high = local_span(rows)
    columns = [
        jnp.concatenate([ops[0, 2 * k + i - RIM] for k in range(low, high)], axis=0)
        for i in range(4)
    ]
    acc[low * pairs : high * pairs] += jnp.dot(
        jnp.concatenate(columns, axis=1),
        two_row_weight(w_ref, 0),
        preferred_element_type=F32,
    )


def finish_kernel(
    info, shifts, acc_in, ops, halo_one, halo_two, w_ref,
    out, send_one, send_two, window, currents, middles, acc, padded, first_step,
):
    parts, rows, pairs, _ = ops.shape
    lanes = halo_one.shape[-1]
    masks = neighbour_masks(pairs, lanes)
    odd_mask = odd_lanes(pairs, lanes)
    even = info[0] == 1
    above_ok = info[1] == 1
    below_ok = info[2] == 1
    keep_latest = info[3] == 1
    if first_step:
        marks = parts * RIM
        above_shift = scalars_of(jnp.where(even, halo_two[marks], halo_one[marks]))
        below_shift = scalars_of(jnp.where(even, halo_one[marks], halo_two[marks]))
    else:
        above_shift = (shifts[0],)
        below_shift = (shifts[1],)
    clear_pads(padded)
    for part in range(parts):
        base = part * RIM

        def own(r, _):
            window[part, RIM + r] = ops[part, r]
            return 0

        lax.fori_loop(0, rows, own, 0, unroll=2)
        warped = part < 2
        for first, near, far, ok, shift in (
            (0, halo_two, halo_one, above_ok, above_shift),
            (RIM + rows, halo_one, halo_two, below_ok, below_shift),
        ):
            if warped:

                def stage(r, _):
                    row = jnp.where(even, near[base + r], far[base + r]).astype(F32)
                    padded[r, PAD : PAD + pairs, :] = jnp.where(ok & keep_latest, row, 0.0)
                    return 0

                lax.fori_loop(0, RIM, stage, 0)

                def warp(r, _):
                    put(
                        window,
                        (part, first + r),
                        fetch_shift(padded, r, shift[part], odd_mask),
                        masks,
                    )
                    return 0

                lax.fori_loop(0, RIM, warp, 0)
            else:

                def plain(r, _):
                    row = jnp.where(even, near[base + r], far[base + r]).astype(F32)
                    put(window, (part, first + r), jnp.where(ok, row, 0.0), masks)
                    return 0

                lax.fori_loop(0, RIM, plain, 0)

    count = (rows + 2 * RIM - 2) // 2
    low, high = local_span(rows)
    low_rows = low * pairs
    high_rows = high * pairs
    for part in range(parts):
        weight = two_row_weight(w_ref, part)
        top = two_row_conv(window.at[part], 0, low, weight)
        bottom = two_row_conv(window.at[part], high, count - high, weight)
        if part > 0:
            acc[0:low_rows] += top
            acc[high_rows : count * pairs] += bottom
        elif first_step:
            acc[0:low_rows] = top
            acc[high_rows : count * pairs] = bottom
        else:
            acc[0:low_rows] = acc_in[0:low_rows] + top
            acc[high_rows : count * pairs] = acc_in[high_rows : count * pairs] + bottom
    acc[low_rows:high_rows] = acc_in[low_rows:high_rows]

    def layer_end(made, margin, function, target):
        def body(k, _):
            both = acc[pl.ds(pl.multiple_of(k * pairs, pairs), pairs), :]
            for q in range(2):
                r = 2 * k + q
                inside = ((r >= margin) | above_ok) & ((r < margin + rows) | below_ok)
                row = function(both[:, q * lanes : (q + 1) * lanes], r).astype(BF16)
                put(target, (r,), jnp.where(inside, row.astype(F32), 0.0), masks)
            return 0

        lax.fori_loop(0, made // 2, body, 0, unroll=2 if made % 4 == 0 else 1)

    def leaky(value, r):
        return jnp.where(value >= 0, value, 0.1 * value)

    def rectified(value, r):
        return jnp.maximum(value, 0.0)

    margin = RIM - 1
    layer_end(rows + 2 * margin, margin, leaky, currents[0])
    for block in range(RES_BLOCKS):
        source = currents[block]
        middle = middles[block]
        margin -= 1
        made = rows + 2 * margin
        acc[0 : made // 2 * pairs] = two_row_conv(
            source, 0, made // 2, two_row_weight(w_ref, 3 + 2 * block)
        )
        layer_end(made, margin, rectified, middle)
        margin -= 1
        made = rows + 2 * margin
        acc[0 : made // 2 * pairs] = two_row_conv(
            middle, 0, made // 2, two_row_weight(w_ref, 4 + 2 * block)
        )

        def added(value, r):
            return value + source[r + 2, :, 0:lanes].astype(F32)

        if block + 1 < RES_BLOCKS:
            layer_end(made, margin, added, currents[block + 1])
        else:
            for k in range(rows // 2):
                both = acc[k * pairs : (k + 1) * pairs, :]
                for q in range(2):
                    r = 2 * k + q
                    row = added(both[:, q * lanes : (q + 1) * lanes], r).astype(BF16)
                    out[r] = row
    if send_one is not None:
        first = slice(0, RIM)
        last = slice(rows - RIM, rows)

        @pl.when(even)
        def _():
            send_one[...] = out[last]
            send_two[...] = out[first]

        @pl.when(jnp.logical_not(even))
        def _():
            send_one[...] = out[first]
            send_two[...] = out[last]


def pair_weights(weight):
    before, here, after = weight[:, :, 0], weight[:, :, 1], weight[:, :, 2]
    zero = jnp.zeros_like(here)
    return jnp.concatenate(
        [
            jnp.concatenate([here, before], axis=-1),
            jnp.concatenate([after, here], axis=-1),
            jnp.concatenate([zero, after], axis=-1),
            jnp.concatenate([before, zero], axis=-1),
        ],
        axis=2,
    )


def shards(features, carried, flow_shift, clip_start, join_weight, res_weight):
    rows = features.shape[1]
    wide = features.shape[2]
    channels = join_weight.shape[2]
    lanes = 2 * channels
    pairs = wide // lanes
    slots = lax.axis_size("rows")
    bands = slots // SECTIONS
    lead = bands // 2
    position = (lax.axis_index("rows") - lead) % slots
    band = position % bands
    owner = position // bands
    even = band % 2 == 0

    def route(move):
        return [(i, move(i) % slots) for i in range(slots)]

    def is_even(i):
        return (i - lead) % 2 == 0

    swap_one = route(lambda i: i + 1 if is_even(i) else i - 1)
    swap_two = route(lambda i: i - 1 if is_even(i) else i + 1)

    def shift_by(count):
        return route(lambda i: i + count)

    def send(block, path):
        return lax.ppermute(block, "rows", path)

    def starts(tick):
        return jnp.sum(
            jnp.where(jnp.arange(SECTIONS) == (owner + tick) % SECTIONS, clip_start, 0)
        ) != tick

    keep = [starts(t) for t in range(TICKS)]
    own_shift = flow_shift[0, 0]

    def info_of(tick):
        keep_earlier = keep[tick] if tick == 0 else keep[tick] & keep[tick - 1]
        values = [
            even, band > 0, band < bands - 1, keep[tick], keep_earlier, own_shift[0], own_shift[1], 0,
        ]
        return jnp.stack([jnp.asarray(v).astype(jnp.int32) for v in values])

    infos = [info_of(t) for t in range(TICKS)]

    carried_rows = carried.reshape(2, rows, pairs, lanes)
    feature_rows = features.reshape(TICKS, rows, pairs, lanes)
    marks = jnp.repeat(flow_shift[:, 0, :].astype(BF16), pairs // 2, axis=1)
    marks = jnp.broadcast_to(marks[:, None, :, None], (TICKS, 1, pairs, lanes))
    own = jnp.concatenate([carried_rows, feature_rows[0:1]], axis=0)
    begin_one = jnp.where(even, rows - RIM, 0)
    begin_two = jnp.where(even, 0, rows - RIM)

    def first_send(begin):
        picked = lax.dynamic_slice_in_dim(own, begin, RIM, axis=1)
        return jnp.concatenate([picked.reshape(3 * RIM, pairs, lanes), marks[0]], axis=0)

    halo_one = send(first_send(begin_one), swap_one)
    halo_two = send(first_send(begin_two), swap_two)

    weights = jnp.concatenate(
        [
            pair_weights(
                join_weight.reshape(3, 3, 3, channels, channels).transpose(2, 0, 1, 3, 4)
            ),
            pair_weights(res_weight.reshape(2 * RES_BLOCKS, 3, 3, channels, channels)),
        ],
        axis=0,
    )

    feats = []
    for tick in range(1, TICKS):
        framed = jnp.concatenate([marks[tick], feature_rows[tick], marks[tick]], axis=0)
        feats.append(send(framed, shift_by(-bands * tick)))
    feats = jnp.stack(feats)
    feats_one = send(
        lax.dynamic_slice_in_dim(feats, jnp.where(even, rows - RIM + 1, 0), RIM + 1, axis=1),
        swap_one,
    )
    feats_two = send(
        lax.dynamic_slice_in_dim(feats, jnp.where(even, 0, rows - RIM + 1), RIM + 1, axis=1),
        swap_two,
    )

    made = rows + 2 * (RIM - 1)
    total = made // 2 * pairs
    acc_type = jax.ShapeDtypeStruct((total, 2 * lanes), F32)
    window_rows = rows + 2 * RIM

    def start():
        return pl.pallas_call(
            start_kernel,
            out_shape=(acc_type, jax.ShapeDtypeStruct((3, rows, pairs, 2 * lanes), BF16)),
            in_specs=[SMEM, VMEM, VMEM],
            out_specs=(VMEM, VMEM),
            scratch_shapes=[pltpu.VMEM((rows, pairs + 2 * PAD, lanes), F32)],
            name="start",
        )(infos[0], own, weights)

    def ahead(tick, latest, prev, prev_one, prev_two):
        def kernel(*refs):
            ahead_kernel(*refs, first_step=False)

        return pl.pallas_call(
            kernel,
            out_shape=(
                acc_type,
                jax.ShapeDtypeStruct((1, rows, pairs, 2 * lanes), BF16),
                jax.ShapeDtypeStruct((2,), jnp.int32),
            ),
            in_specs=[SMEM] + [VMEM] * 8,
            out_specs=(VMEM, VMEM, SMEM),
            scratch_shapes=[
                pltpu.VMEM((window_rows, pairs + 2 * PAD, lanes), F32),
                pltpu.VMEM((2, window_rows, pairs, 2 * lanes), BF16),
            ],
            name=f"ahead_{tick}",
        )(
            infos[tick], latest, prev, prev_one, prev_two,
            feats[tick - 1], feats_one[tick - 1], feats_two[tick - 1], weights,
        )

    def finish(tick, shifts, acc, ops, one, two):
        last = tick + 1 == TICKS
        parts = ops.shape[0]

        def kernel(info, shifts, acc_in, ops, one, two, w_ref, *rest):
            if last:
                out, *scratch = rest
                send_one = send_two = None
            else:
                out, send_one, send_two, *scratch = rest
            window, cur_0, cur_1, mid_0, mid_1, acc, padded = scratch
            finish_kernel(
                info, shifts, acc_in, ops, one, two, w_ref, out, send_one, send_two,
                window, (cur_0, cur_1), (mid_0, mid_1), acc, padded, tick == 0,
            )

        block = jax.ShapeDtypeStruct((rows, pairs, lanes), BF16)
        halo = jax.ShapeDtypeStruct((RIM, pairs, lanes), BF16)
        outs = (block,) if last else (block, halo, halo)

        def rows_of(count):
            return pltpu.VMEM((count, pairs, 2 * lanes), BF16)

        return pl.pallas_call(
            kernel,
            out_shape=outs,
            in_specs=[SMEM, SMEM] + [VMEM] * 5,
            out_specs=tuple(VMEM for _ in outs),
            scratch_shapes=[
                pltpu.VMEM((parts, window_rows, pairs, 2 * lanes), BF16),
                rows_of(rows + 8), rows_of(rows + 4), rows_of(rows + 6), rows_of(rows + 2),
                pltpu.VMEM((total, 2 * lanes), F32),
                pltpu.VMEM((RIM, pairs + 2 * PAD, lanes), F32),
            ],
            name=f"finish_{tick}",
        )(infos[tick], shifts, acc, ops, one, two, weights)

    results = []
    acc, ops = start()
    latest, send_one, send_two = finish(0, jnp.zeros((2,), jnp.int32), acc, ops, halo_one, halo_two)
    results.append(latest)
    prev, prev_one, prev_two = carried_rows[0], halo_one, halo_two
    for tick in range(1, TICKS):
        one = send(send_one, swap_one)
        two = send(send_two, swap_two)
        acc, ops, shifts = ahead(tick, latest, prev, prev_one, prev_two)
        prev, prev_one, prev_two = latest, one, two
        outs = finish(tick, shifts, acc, ops, one, two)
        latest = outs[0]
        if tick + 1 < TICKS:
            send_one, send_two = outs[1:]
        results.append(send(latest, shift_by(bands * tick)))
    return jnp.stack([r.reshape(rows, wide) for r in results])


def solution(mesh):
    in_specs = (
        P(None, ("groups", "rows"), None),
        P(None, ("groups", "rows"), None),
        P(None, ("groups", "rows"), None),
        P("groups"),
        P(),
        P(),
    )
    out_specs = P(None, ("groups", "rows"), None)
    return jax.shard_map(shards, mesh=mesh, in_specs=in_specs, out_specs=out_specs, check_vma=False)
```

```python
import jax
import jax.numpy as jnp
from jax import lax
from jax.experimental import pallas as pl
from jax.experimental.pallas import tpu as pltpu
from jax.sharding import PartitionSpec as P

TICKS = 3
SECTIONS = 4
RES_BLOCKS = 2
MAXSHIFT = 8
RIM = 1 + 2 * RES_BLOCKS
PAD = 8
SUB = 8
GRANT = 24 << 20

BF16 = jnp.bfloat16
F32 = jnp.float32
VMEM = pl.BlockSpec(memory_space=pltpu.VMEM)
SMEM = pl.BlockSpec(memory_space=pltpu.SMEM)


def lane_low(lanes):
    return lax.broadcasted_iota(jnp.int32, (SUB, lanes), 1) < lanes // 2


def sublane(lanes):
    return lax.broadcasted_iota(jnp.int32, (SUB, lanes), 0)


def store_operand(dst, index, groups, low):
    here = jnp.concatenate(groups[1:-1], axis=0)
    beside = jnp.concatenate(
        [jnp.where(low, groups[v + 2], groups[v]) for v in range(len(groups) - 2)], axis=0
    )
    dst[index + (0,)] = here.astype(BF16)
    dst[index + (1,)] = beside.astype(BF16)


def put(dst, index, row, low, sub):
    count = row.shape[0] // SUB
    groups = [row[SUB * v : SUB * v + SUB] for v in range(count)]
    before = jnp.where(sub > 0, pltpu.roll(groups[-1], 1, 0), 0.0)
    after = jnp.where(sub < SUB - 1, pltpu.roll(groups[0], SUB - 1, 0), 0.0)
    store_operand(dst, index, [before] + groups + [after], low)


def stage(padded, row, value, interleaved):
    pairs = value.shape[0]
    count = pairs // SUB
    if interleaved:
        for v in range(count):
            padded[row, pl.ds(PAD + v, SUB, stride=count), :] = value[SUB * v : SUB * v + SUB]
    else:
        padded[row, PAD : PAD + pairs, :] = value


def put_plain(dst, index, padded, row, low):
    count = (padded.shape[1] - 2 * PAD) // SUB
    groups = [
        padded[row, pl.ds(PAD + v, SUB, stride=count), :] for v in range(-1, count + 1)
    ]
    store_operand(dst, index, groups, low)


def put_warped(dst, index, padded, row, shift, low, sub):
    count = (padded.shape[1] - 2 * PAD) // SUB
    lanes = padded.shape[2]
    start = PAD - (shift >> 1)
    is_odd = (shift & 1) == 1
    raw = [
        padded[row, pl.ds(start + v, SUB, stride=count), :] for v in range(-2, count + 1)
    ]
    groups = []
    for v in range(1, len(raw)):
        odd = pltpu.roll(jnp.where(low, raw[v], raw[v - 1]), lanes // 2, 1)
        groups.append(jnp.where(is_odd, odd, raw[v]))
    groups[0] = jnp.where(sub > 0, groups[0], 0.0)
    groups[-1] = jnp.where(sub < SUB - 1, groups[-1], 0.0)
    store_operand(dst, index, groups, low)


def two_row_weight(w_ref, layers):
    rows = []
    for layer in layers:
        zero = jnp.zeros(w_ref.shape[2:], BF16)
        w = [w_ref[layer, a] for a in range(3)]
        for pair in ((w[0], zero), (w[1], w[0]), (w[2], w[1]), (zero, w[2])):
            rows.append(jnp.concatenate(pair, axis=1))
    return jnp.concatenate(rows, axis=0)


def two_row_conv(fetches, first, count, w_ref, layers):
    columns = []
    for fetch in fetches:
        for i in range(4):
            for part in range(2):
                columns.append(
                    jnp.concatenate(
                        [fetch(2 * (first + k) + i, part) for k in range(count)], axis=0
                    )
                )
    return jnp.dot(
        jnp.concatenate(columns, axis=1),
        two_row_weight(w_ref, layers),
        preferred_element_type=F32,
    )


def scalars_of(row):
    half = row.shape[0] // 2
    wide = row.astype(F32)
    return (
        jnp.max(wide[0:SUB]).astype(jnp.int32),
        jnp.max(wide[half : half + SUB]).astype(jnp.int32),
    )


def local_span(band_rows):
    return (RIM + 1) // 2, (RIM + band_rows - 4) // 2 + 1


def clear_pads(padded):
    rows, long, lanes = padded.shape
    for row in range(rows):
        padded[row, 0:PAD, :] = jnp.zeros((PAD, lanes), F32)
        padded[row, long - PAD :, :] = jnp.zeros((PAD, lanes), F32)


class Place:
    def __init__(self, index, clip, slots):
        bands = slots // SECTIONS
        position = lax.rem(index[0] + (slots - bands // 2), slots)
        self.band = lax.rem(position, bands)
        self.owner = lax.div(position, bands)
        self.clip = clip
        self.even = lax.rem(self.band, 2) == 0
        self.above = self.band > 0
        self.below = self.band < bands - 1

    def keep(self, tick):
        return self.clip[lax.rem(self.owner + tick, SECTIONS)] != tick


def start_kernel(slots, index, clip, flow, carried, feature, w_ref, acc, ops, padded):
    _, rows, pairs, lanes = carried.shape
    place = Place(index, clip, slots)
    low, sub = lane_low(lanes), sublane(lanes)
    clear_pads(padded)
    keep = place.keep(0)
    for part in range(2):
        for r in range(rows):
            stage(padded, part * rows + r, jnp.where(keep, carried[part, r].astype(F32), 0.0), False)
            put_warped(ops, (part, r), padded, part * rows + r, flow[0, 0, part], low, sub)
    for r in range(rows):
        stage(padded, 2 * rows + r, feature[r].astype(F32), False)
        put_plain(ops, (2, r), padded, 2 * rows + r, low)
    first, end = local_span(rows)
    fetches = [lambda r, h, part=part: ops[part, r - RIM, h] for part in range(3)]
    acc[...] = two_row_conv(fetches, first, end - first, w_ref, (0, 1, 2))


def ahead_kernel(
    slots, tick, interleaved, index, clip, latest, prev, prev_one, prev_two,
    feat, feat_above, feat_below, w_ref, acc, ops, shifts, padded, padded_latest, window,
):
    rows, pairs, lanes = latest.shape
    place = Place(index, clip, slots)
    even = place.even
    low, sub = lane_low(lanes), sublane(lanes)
    keep_latest = place.keep(tick)
    keep_earlier = keep_latest & place.keep(tick - 1)
    own_shift = scalars_of(feat[0])
    above_shift = scalars_of(feat_above[RIM])
    below_shift = scalars_of(feat_below[0])
    shifts[0] = above_shift[0]
    shifts[1] = below_shift[0]
    clear_pads(padded)
    clear_pads(padded_latest)
    span = rows + 2 * RIM
    for r in range(span):
        if r < RIM:
            row, ok = feat_above[r].astype(F32), place.above
        elif r < RIM + rows:
            row, ok = feat[1 + r - RIM].astype(F32), None
        else:
            row, ok = feat_below[1 + r - RIM - rows].astype(F32), place.below
        stage(padded, r, row if ok is None else jnp.where(ok, row, 0.0), False)
        put_plain(window, (1, r), padded, r, low)
    for r in range(span):
        at = span + r
        if r < RIM:
            row = jnp.where(even, prev_two[r], prev_one[r])
            ok, shift = place.above & keep_earlier, above_shift[1]
        elif r < RIM + rows:
            row = prev[r - RIM]
            ok, shift = keep_earlier, own_shift[1]
        else:
            q = r - RIM - rows
            row = jnp.where(even, prev_one[q], prev_two[q])
            ok, shift = place.below & keep_earlier, below_shift[1]
        stage(padded, at, jnp.where(ok, row.astype(F32), 0.0), interleaved)
        put_warped(window, (0, r), padded, at, shift, low, sub)
    for r in range(rows):
        stage(padded_latest, r, jnp.where(keep_latest, latest[r].astype(F32), 0.0), True)
        put_warped(ops, (0, r), padded_latest, r, own_shift[0], low, sub)
    count = (span - 2) // 2
    first, end = local_span(rows)
    known = [lambda r, h: window[0, r, h], lambda r, h: window[1, r, h]]
    latest_own = [lambda r, h: ops[0, r - RIM, h]]
    for begin, stop, fetches, layers in (
        (0, first, known, (1, 2)),
        (first, end, latest_own + known, (0, 1, 2)),
        (end, count, known, (1, 2)),
    ):
        acc[begin * pairs : stop * pairs] = two_row_conv(
            fetches, begin, stop - begin, w_ref, layers
        )


def finish_kernel(
    slots, tick, index, clip, shifts, acc_in, ops, halo_one, halo_two, w_ref,
    latest, natural, sends, window, layers, padded, plain_rows,
):
    parts, rows, _, pairs, lanes = ops.shape
    place = Place(index, clip, slots)
    even = place.even
    low, sub = lane_low(lanes), sublane(lanes)
    keep = place.keep(tick)
    if tick == 0:
        marks = parts * RIM
        above_shift = scalars_of(jnp.where(even, halo_two[marks], halo_one[marks]))
        below_shift = scalars_of(jnp.where(even, halo_one[marks], halo_two[marks]))
    else:
        above_shift = (shifts[0],)
        below_shift = (shifts[1],)
    clear_pads(padded)
    order = [("above", r) for r in range(RIM)] + [("below", r) for r in range(RIM)]
    at = 0
    for where, r in order:
        for part in range(parts):
            near, far = (halo_two, halo_one) if where == "above" else (halo_one, halo_two)
            ok = place.above if where == "above" else place.below
            shift = above_shift if where == "above" else below_shift
            slot = r if where == "above" else RIM + r
            row = jnp.where(even, near[part * RIM + r], far[part * RIM + r]).astype(F32)
            if part < 2:
                ok = ok & keep
            stage(padded, at, jnp.where(ok, row, 0.0), tick > 0)
            if part < 2:
                put_warped(window, (part, slot), padded, at, shift[part], low, sub)
            else:
                put_plain(window, (part, slot), padded, at, low)
            at += 1

    def operand(part):
        def fetch(r, h):
            if r < RIM:
                return window[part, r, h]
            if r < RIM + rows:
                return ops[part, r - RIM, h]
            return window[part, r - rows, h]

        return fetch

    count = (rows + 2 * RIM - 2) // 2
    first, end = local_span(rows)
    split = end

    def emit(layer, pair, both):
        margin = RIM - 1 - layer
        for q in range(2):
            r = 2 * pair + q
            value = both[:, q * lanes : (q + 1) * lanes]
            if layer == 0:
                value = jnp.maximum(value, 0.1 * value)
            elif layer % 2 == 1:
                value = jnp.maximum(value, 0.0)
            else:
                value = value + layers[layer - 2][r + 2, 0].astype(F32)
            if r < margin:
                value = jnp.where(place.above, value, 0.0)
            elif r >= margin + rows:
                value = jnp.where(place.below, value, 0.0)
            if layer < 2 * RES_BLOCKS:
                put(layers[layer], (r,), value, low, sub)
            else:
                plain_rows[r] = value
                if latest is not None:
                    latest[r] = value.astype(BF16)

    fetches = [operand(part) for part in range(parts)]
    join = tuple(range(parts))
    for begin, stop in ((0, first), (first, end), (end, count)):
        made = None
        if begin != first:
            made = two_row_conv(fetches, begin, stop - begin, w_ref, join)
        for k in range(begin, stop):
            if begin == first:
                at = k - first if tick == 0 else k
                both = acc_in[at * pairs : (at + 1) * pairs]
            else:
                both = made[(k - begin) * pairs : (k - begin + 1) * pairs]
                if tick > 0:
                    both = both + acc_in[k * pairs : (k + 1) * pairs]
            emit(0, k, both)
    for layer in range(1, 2 * RES_BLOCKS + 1):
        count -= 1
        split -= 1
        for begin, stop in ((0, split), (split, count)):
            made = two_row_conv(
                [lambda r, h: layers[layer - 1][r, h]], begin, stop - begin, w_ref, (2 + layer,)
            )
            for k in range(begin, stop):
                emit(layer, k, made[(k - begin) * pairs : (k - begin + 1) * pairs])
    groups = pairs // SUB
    flat = plain_rows.reshape(rows * pairs, lanes)
    for v in range(groups):
        for s in range(SUB):
            pair = groups * s + v
            tile = flat[pl.ds(SUB * v + s, rows, stride=pairs), :]
            natural[:, pair * lanes : (pair + 1) * lanes] = tile.astype(BF16)
    if sends:
        send_one, send_two = sends

        @pl.when(even)
        def _():
            send_one[...] = latest[rows - RIM : rows]
            send_two[...] = latest[0:RIM]

        @pl.when(jnp.logical_not(even))
        def _():
            send_one[...] = latest[0:RIM]
            send_two[...] = latest[rows - RIM : rows]


def pair_weights(weight):
    before, here, after = weight[:, :, 0], weight[:, :, 1], weight[:, :, 2]
    zero = jnp.zeros_like(here)
    return jnp.concatenate(
        [
            jnp.concatenate([here, before], axis=-1),
            jnp.concatenate([after, here], axis=-1),
            jnp.concatenate([zero, after], axis=-1),
            jnp.concatenate([before, zero], axis=-1),
        ],
        axis=2,
    )


def shards(features, carried, flow_shift, clip_start, join_weight, res_weight):
    rows = features.shape[1]
    wide = features.shape[2]
    channels = join_weight.shape[2]
    lanes = 2 * channels
    pairs = wide // lanes
    slots = lax.axis_size("rows")
    bands = slots // SECTIONS
    lead = bands // 2
    index = lax.axis_index("rows")
    even = (index + (slots - lead)) % 2 == 0
    index = index.astype(jnp.int32).reshape(1)

    def route(move):
        return [(i, move(i) % slots) for i in range(slots)]

    def is_even(i):
        return (i - lead) % 2 == 0

    swap_one = route(lambda i: i + 1 if is_even(i) else i - 1)
    swap_two = route(lambda i: i - 1 if is_even(i) else i + 1)

    def shift_by(count):
        return route(lambda i: i + count)

    def send(block, path):
        return lax.ppermute(block, "rows", path)

    marks = jnp.repeat(flow_shift[:, 0, :].astype(BF16), pairs // 2, axis=1)
    marks = jnp.broadcast_to(marks[:, None, :, None], (TICKS, 1, pairs, lanes))
    carried_rows = carried.reshape(2, rows, pairs, lanes)
    feature_rows = features[0].reshape(rows, pairs, lanes)

    def first_send(begin):
        picked = [
            lax.dynamic_slice_in_dim(block, begin, RIM, axis=0)
            for block in (carried_rows[0], carried_rows[1], feature_rows)
        ]
        return jnp.concatenate(picked + [marks[0]], axis=0)

    first_one = first_send(jnp.where(even, rows - RIM, 0))
    first_two = first_send(jnp.where(even, 0, rows - RIM))
    later_features, marks, first_one, first_two = lax.optimization_barrier(
        (features[1:], marks, first_one, first_two)
    )
    halo_one = send(first_one, swap_one)
    halo_two = send(first_two, swap_two)

    feats = []
    for tick in range(1, TICKS):
        framed = jnp.concatenate(
            [marks[tick], later_features[tick - 1].reshape(rows, pairs, lanes), marks[tick]], axis=0
        )
        back = -bands * tick
        feats.append(
            (
                send(framed, shift_by(back)),
                send(framed[rows + 1 - RIM :], shift_by(back + 1)),
                send(framed[: RIM + 1], shift_by(back - 1)),
            )
        )

    weights = jnp.concatenate(
        [
            pair_weights(
                join_weight.reshape(3, 3, 3, channels, channels).transpose(2, 0, 1, 3, 4)
            ),
            pair_weights(res_weight.reshape(2 * RES_BLOCKS, 3, 3, channels, channels)),
        ],
        axis=0,
    )

    made = rows + 2 * (RIM - 1)
    total = made // 2 * pairs
    span = rows + 2 * RIM
    long = pairs + 2 * PAD
    first, end = local_span(rows)
    params = pltpu.CompilerParams(vmem_limit_bytes=GRANT)

    def cost(pairs_done, depth):
        return pl.CostEstimate(
            flops=pairs_done * pairs * depth * 16 * lanes * lanes,
            bytes_accessed=4 << 20,
            transcendentals=0,
        )

    def operands(*lead_shape):
        return lead_shape + (2, pairs, lanes)

    def start():
        def kernel(*refs):
            start_kernel(slots, *refs)

        return pl.pallas_call(
            kernel,
            out_shape=(
                jax.ShapeDtypeStruct(((end - first) * pairs, 2 * lanes), F32),
                jax.ShapeDtypeStruct(operands(3, rows), BF16),
            ),
            in_specs=[SMEM, SMEM, SMEM, VMEM, VMEM, VMEM],
            out_specs=(VMEM, VMEM),
            scratch_shapes=[pltpu.VMEM((3 * rows, long, lanes), F32)],
            compiler_params=params,
            cost_estimate=cost(end - first, 3),
            name="start",
        )(index, clip_start, flow_shift, carried_rows, feature_rows, weights)

    def ahead(tick, latest, prev, prev_one, prev_two):
        def kernel(*refs):
            ahead_kernel(slots, tick, tick > 1, *refs)

        return pl.pallas_call(
            kernel,
            out_shape=(
                jax.ShapeDtypeStruct((total, 2 * lanes), F32),
                jax.ShapeDtypeStruct(operands(1, rows), BF16),
                jax.ShapeDtypeStruct((2,), jnp.int32),
            ),
            in_specs=[SMEM, SMEM] + [VMEM] * 8,
            out_specs=(VMEM, VMEM, SMEM),
            scratch_shapes=[
                pltpu.VMEM((2 * span, long, lanes), F32),
                pltpu.VMEM((rows, long, lanes), F32),
                pltpu.VMEM(operands(2, span), BF16),
            ],
            compiler_params=params,
            cost_estimate=cost(made, 1),
            name=f"ahead_{tick}",
        )(index, clip_start, latest, prev, prev_one, prev_two, *feats[tick - 1], weights)

    def finish(tick, shifts, acc, ops, one, two):
        last = tick + 1 == TICKS
        parts = ops.shape[0]

        def kernel(index, clip, shifts, acc_in, ops, one, two, w_ref, *rest):
            if last:
                natural, *scratch = rest
                latest, sends = None, ()
            else:
                natural, latest, send_one, send_two, *scratch = rest
                sends = (send_one, send_two)
            window, *layers, padded, plain_rows = scratch
            finish_kernel(
                slots, tick, index, clip, shifts, acc_in, ops, one, two, w_ref,
                latest, natural, sends, window, layers, padded, plain_rows,
            )

        halo = jax.ShapeDtypeStruct((RIM, pairs, lanes), BF16)
        outs = (jax.ShapeDtypeStruct((rows, wide), BF16),)
        if not last:
            outs += (jax.ShapeDtypeStruct((rows, pairs, lanes), BF16), halo, halo)
        return pl.pallas_call(
            kernel,
            out_shape=outs,
            in_specs=[SMEM, SMEM, SMEM] + [VMEM] * 5,
            out_specs=tuple(VMEM for _ in outs),
            scratch_shapes=[pltpu.VMEM(operands(parts, 2 * RIM), BF16)]
            + [pltpu.VMEM(operands(made - 2 * layer), BF16) for layer in range(2 * RES_BLOCKS)]
            + [
                pltpu.VMEM((parts * 2 * RIM, long, lanes), F32),
                pltpu.VMEM((rows, pairs, lanes), F32),
            ],
            compiler_params=params,
            cost_estimate=cost(made + made // 2 * parts, 1),
            name=f"finish_{tick}",
        )(index, clip_start, shifts, acc, ops, one, two, weights)

    results = []
    acc, ops = start()
    natural, latest, send_one, send_two = finish(
        0, flow_shift[0, 0], acc, ops, halo_one, halo_two
    )
    results.append(natural)
    prev, prev_one, prev_two = carried_rows[0], halo_one, halo_two
    for tick in range(1, TICKS):
        one = send(send_one, swap_one)
        two = send(send_two, swap_two)
        acc, ops, shifts = ahead(tick, latest, prev, prev_one, prev_two)
        prev, prev_one, prev_two = latest, one, two
        natural, *rest = finish(tick, shifts, acc, ops, one, two)
        if tick + 1 < TICKS:
            latest, send_one, send_two = rest
        results.append(send(natural, shift_by(bands * tick)))
    return jnp.stack(results)


def solution(mesh):
    in_specs = (
        P(None, ("groups", "rows"), None),
        P(None, ("groups", "rows"), None),
        P(None, ("groups", "rows"), None),
        P("groups"),
        P(),
        P(),
    )
    out_specs = P(None, ("groups", "rows"), None)
    return jax.shard_map(shards, mesh=mesh, in_specs=in_specs, out_specs=out_specs, check_vma=False)
```

```python
import jax
import jax.numpy as jnp
from jax import lax
from jax.experimental import pallas as pl
from jax.experimental.pallas import tpu as pltpu
from jax.sharding import PartitionSpec as P


TICKS = 3
SECTIONS = 4
RES_BLOCKS = 2
RIM = 1 + 2 * RES_BLOCKS
PAD = 8
SUB = 8
GRANT = 24 << 20

BF16 = jnp.bfloat16
F32 = jnp.float32
VMEM = pl.BlockSpec(memory_space=pltpu.VMEM)
SMEM = pl.BlockSpec(memory_space=pltpu.SMEM)
HBM = pl.BlockSpec(memory_space=pltpu.HBM)


def in_hbm(block):
    return pltpu.with_memory_space_constraint(block, pltpu.HBM)


def lane_low(lanes):
    return lax.broadcasted_iota(jnp.int32, (SUB, lanes), 1) < lanes // 2


def sublane(lanes):
    return lax.broadcasted_iota(jnp.int32, (SUB, lanes), 0)


def store_operand(dst, index, groups, low):
    here = jnp.concatenate(groups[1:-1], axis=0)
    beside = jnp.concatenate(
        [jnp.where(low, groups[v + 2], groups[v]) for v in range(len(groups) - 2)], axis=0
    )
    dst[index + (0,)] = here.astype(BF16)
    dst[index + (1,)] = beside.astype(BF16)


def put(dst, index, row, low, sub):
    count = row.shape[0] // SUB
    groups = [row[SUB * v : SUB * v + SUB] for v in range(count)]
    before = jnp.where(sub > 0, pltpu.roll(groups[-1], 1, 0), 0.0)
    after = jnp.where(sub < SUB - 1, pltpu.roll(groups[0], SUB - 1, 0), 0.0)
    store_operand(dst, index, [before] + groups + [after], low)


def stage(padded, row, value, interleaved):
    pairs = value.shape[0]
    count = pairs // SUB
    if interleaved:
        for v in range(count):
            padded[row, pl.ds(PAD + v, SUB, stride=count), :] = value[SUB * v : SUB * v + SUB]
    else:
        padded[row, PAD : PAD + pairs, :] = value


def put_plain(dst, index, padded, row, low):
    count = (padded.shape[1] - 2 * PAD) // SUB
    groups = [
        padded[row, pl.ds(PAD + v, SUB, stride=count), :] for v in range(-1, count + 1)
    ]
    store_operand(dst, index, groups, low)


def put_warped(dst, index, padded, row, shift, low, sub):
    count = (padded.shape[1] - 2 * PAD) // SUB
    lanes = padded.shape[2]
    start = PAD - (shift >> 1)
    is_odd = (shift & 1) == 1
    raw = [
        padded[row, pl.ds(start + v, SUB, stride=count), :] for v in range(-2, count + 1)
    ]
    groups = []
    for v in range(1, len(raw)):
        odd = pltpu.roll(jnp.where(low, raw[v], raw[v - 1]), lanes // 2, 1)
        groups.append(jnp.where(is_odd, odd, raw[v]))
    groups[0] = jnp.where(sub > 0, groups[0], 0.0)
    groups[-1] = jnp.where(sub < SUB - 1, groups[-1], 0.0)
    store_operand(dst, index, groups, low)


def two_row_weight(w_ref, layers):
    rows = []
    for layer in layers:
        zero = jnp.zeros(w_ref.shape[2:], BF16)
        w = [w_ref[layer, a] for a in range(3)]
        for pair in ((w[0], zero), (w[1], w[0]), (w[2], w[1]), (zero, w[2])):
            rows.append(jnp.concatenate(pair, axis=1))
    return jnp.concatenate(rows, axis=0)


def two_row_conv(fetches, first, count, w_ref, layers):
    columns = []
    for fetch in fetches:
        for i in range(4):
            for part in range(2):
                columns.append(
                    jnp.concatenate(
                        [fetch(2 * (first + k) + i, part) for k in range(count)], axis=0
                    )
                )
    return jnp.dot(
        jnp.concatenate(columns, axis=1),
        two_row_weight(w_ref, layers),
        preferred_element_type=F32,
    )


def scalars_of(row):
    half = row.shape[0] // 2
    wide = row.astype(F32)
    return (
        jnp.max(wide[0:SUB]).astype(jnp.int32),
        jnp.max(wide[half : half + SUB]).astype(jnp.int32),
    )


def local_span(band_rows):
    return (RIM + 1) // 2, (RIM + band_rows - 4) // 2 + 1


def clear_pads(padded):
    rows, long, lanes = padded.shape
    for row in range(rows):
        padded[row, 0:PAD, :] = jnp.zeros((PAD, lanes), F32)
        padded[row, long - PAD :, :] = jnp.zeros((PAD, lanes), F32)


class Place:
    def __init__(self, index, clip, slots):
        bands = slots // SECTIONS
        position = lax.rem(index[0] + (slots - bands // 2), slots)
        self.band = lax.rem(position, bands)
        self.owner = lax.div(position, bands)
        self.clip = clip
        self.even = lax.rem(self.band, 2) == 0
        self.above = self.band > 0
        self.below = self.band < bands - 1

    def keep(self, tick):
        return self.clip[lax.rem(self.owner + tick, SECTIONS)] != tick


def natural_to_rows(scratch, block):
    rows = block.shape[0]
    lanes = scratch.shape[1]
    pairs = block.shape[1] // lanes
    pitch = scratch.shape[0] // rows
    for p in range(pairs):
        tile = block[:, p * lanes : (p + 1) * lanes].astype(F32)
        scratch[pl.ds(p, rows, stride=pitch), :] = tile
    return [scratch[r * pitch : r * pitch + pairs, :].astype(BF16) for r in range(rows)]


def shift_row(flow, tick, pairs, lanes):
    halves = [
        jnp.full((pairs // 2, lanes), flow[0, which, tick].astype(F32)) for which in range(2)
    ]
    return jnp.concatenate(halves, axis=0).astype(BF16)


def pack_kernel(
    slots, index, flow_in, carried, features, own, first_one, first_two, natural, scratch, sems,
    flow,
):
    _, rows, pairs, lanes = own.shape
    place = Place(index, None, slots)
    copies = [
        pltpu.make_async_copy(block, natural.at[part], sems.at[part])
        for part, block in enumerate((carried.at[0], carried.at[1], features.at[0]))
    ]
    copies.append(pltpu.make_async_copy(flow_in, flow, sems.at[3]))
    for copy in copies:
        copy.start()
    for part in range(3):
        copies[part].wait()
        for r, row in enumerate(natural_to_rows(scratch.at[part], natural.at[part])):
            own[part, r] = row
    copies[3].wait()
    mark = shift_row(flow, 0, pairs, lanes)
    first_one[3 * RIM] = mark
    first_two[3 * RIM] = mark
    for last, first, chosen in (
        (first_one, first_two, place.even),
        (first_two, first_one, jnp.logical_not(place.even)),
    ):

        @pl.when(chosen)
        def _():
            for part in range(3):
                last[part * RIM : (part + 1) * RIM] = own[part, rows - RIM : rows]
                first[part * RIM : (part + 1) * RIM] = own[part, 0:RIM]


def frame_kernel(flow_in, features, *rest):
    *framed, natural, scratch, sems, flow = rest
    _, pairs, lanes = framed[0].shape
    rows = framed[0].shape[0] - 2
    copies = [
        pltpu.make_async_copy(features.at[later + 1], natural.at[later], sems.at[later])
        for later in range(len(framed))
    ]
    copies.append(pltpu.make_async_copy(flow_in, flow, sems.at[len(framed)]))
    for copy in copies:
        copy.start()
    for later, frame in enumerate(framed):
        copies[later].wait()
        for r, row in enumerate(natural_to_rows(scratch.at[later], natural.at[later])):
            frame[1 + r] = row
    copies[-1].wait()
    for later, frame in enumerate(framed):
        mark = shift_row(flow, later + 1, pairs, lanes)
        frame[0] = mark
        frame[rows + 1] = mark


def start_kernel(slots, index, clip, flow, own, w_ref, acc, ops, padded):
    _, rows, _, lanes = own.shape
    place = Place(index, clip, slots)
    low, sub = lane_low(lanes), sublane(lanes)
    clear_pads(padded)
    keep = place.keep(0)
    for part in range(2):
        for r in range(rows):
            stage(padded, part * rows + r, jnp.where(keep, own[part, r].astype(F32), 0.0), False)
            put_warped(ops, (part, r), padded, part * rows + r, flow[0, part, 0], low, sub)
    for r in range(rows):
        stage(padded, 2 * rows + r, own[2, r].astype(F32), False)
        put_plain(ops, (2, r), padded, 2 * rows + r, low)
    first, end = local_span(rows)
    fetches = [lambda r, h, part=part: ops[part, r - RIM, h] for part in range(3)]
    acc[...] = two_row_conv(fetches, first, end - first, w_ref, (0, 1, 2))


def rows_to_natural(natural, plain_rows):
    rows, pairs, lanes = plain_rows.shape
    groups = pairs // SUB
    flat = plain_rows.reshape(rows * pairs, lanes)
    for v in range(groups):
        for s in range(SUB):
            pair = groups * s + v
            tile = flat[pl.ds(SUB * v + s, rows, stride=pairs), :]
            natural[:, pair * lanes : (pair + 1) * lanes] = tile.astype(BF16)


def ahead_kernel(
    slots, tick, interleaved, index, clip, latest, prev, prev_one, prev_two,
    feat, feat_above, feat_below, w_ref, acc, ops, shifts, natural,
    padded, padded_latest, window, plain_rows, *copying,
):
    rows, pairs, lanes = latest.shape
    place = Place(index, clip, slots)
    even = place.even
    low, sub = lane_low(lanes), sublane(lanes)
    keep_latest = place.keep(tick)
    keep_earlier = keep_latest & place.keep(tick - 1)
    own_shift = scalars_of(feat[0])
    above_shift = scalars_of(feat_above[RIM])
    below_shift = scalars_of(feat_below[0])
    shifts[0] = above_shift[0]
    shifts[1] = below_shift[0]
    clear_pads(padded)
    clear_pads(padded_latest)
    span = rows + 2 * RIM
    for r in range(span):
        if r < RIM:
            row, ok = feat_above[r].astype(F32), place.above
        elif r < RIM + rows:
            row, ok = feat[1 + r - RIM].astype(F32), None
        else:
            row, ok = feat_below[1 + r - RIM - rows].astype(F32), place.below
        stage(padded, r, row if ok is None else jnp.where(ok, row, 0.0), False)
        put_plain(window, (1, r), padded, r, low)
    for r in range(span):
        at = span + r
        if r < RIM:
            row = jnp.where(even, prev_two[r], prev_one[r])
            ok, shift = place.above & keep_earlier, above_shift[1]
        elif r < RIM + rows:
            row = prev[r - RIM]
            ok, shift = keep_earlier, own_shift[1]
        else:
            q = r - RIM - rows
            row = jnp.where(even, prev_one[q], prev_two[q])
            ok, shift = place.below & keep_earlier, below_shift[1]
        stage(padded, at, jnp.where(ok, row.astype(F32), 0.0), interleaved)
        put_warped(window, (0, r), padded, at, shift, low, sub)
    for r in range(rows):
        row = latest[r].astype(F32)
        plain_rows[r] = row
        stage(padded_latest, r, jnp.where(keep_latest, row, 0.0), True)
        put_warped(ops, (0, r), padded_latest, r, own_shift[0], low, sub)
    count = (span - 2) // 2
    first, end = local_span(rows)
    known = [lambda r, h: window[0, r, h], lambda r, h: window[1, r, h]]
    latest_own = [lambda r, h: ops[0, r - RIM, h]]
    for begin, stop, fetches, layers in (
        (0, first, known, (1, 2)),
        (first, end, latest_own + known, (0, 1, 2)),
        (end, count, known, (1, 2)),
    ):
        acc[begin * pairs : stop * pairs] = two_row_conv(
            fetches, begin, stop - begin, w_ref, layers
        )
    if copying:
        natural_rows, sem = copying
        rows_to_natural(natural_rows, plain_rows)
        copy = pltpu.make_async_copy(natural_rows, natural.at[0], sem)
        copy.start()
        copy.wait()
    else:
        rows_to_natural(natural, plain_rows)


def finish_kernel(
    slots, tick, index, clip, shifts, acc_in, ops, halo_one, halo_two, w_ref,
    latest, natural, sends, window, layers, padded, plain_rows,
):
    parts, rows, _, pairs, lanes = ops.shape
    place = Place(index, clip, slots)
    even = place.even
    low, sub = lane_low(lanes), sublane(lanes)
    keep = place.keep(tick)
    if tick == 0:
        marks = parts * RIM
        above_shift = scalars_of(jnp.where(even, halo_two[marks], halo_one[marks]))
        below_shift = scalars_of(jnp.where(even, halo_one[marks], halo_two[marks]))
    else:
        above_shift = (shifts[0],)
        below_shift = (shifts[1],)
    clear_pads(padded)
    order = [("above", r) for r in range(RIM)] + [("below", r) for r in range(RIM)]
    at = 0
    for where, r in order:
        for part in range(parts):
            near, far = (halo_two, halo_one) if where == "above" else (halo_one, halo_two)
            ok = place.above if where == "above" else place.below
            shift = above_shift if where == "above" else below_shift
            slot = r if where == "above" else RIM + r
            row = jnp.where(even, near[part * RIM + r], far[part * RIM + r]).astype(F32)
            if part < 2:
                ok = ok & keep
            stage(padded, at, jnp.where(ok, row, 0.0), tick > 0)
            if part < 2:
                put_warped(window, (part, slot), padded, at, shift[part], low, sub)
            else:
                put_plain(window, (part, slot), padded, at, low)
            at += 1

    def operand(part):
        def fetch(r, h):
            if r < RIM:
                return window[part, r, h]
            if r < RIM + rows:
                return ops[part, r - RIM, h]
            return window[part, r - rows, h]

        return fetch

    count = (rows + 2 * RIM - 2) // 2
    first, end = local_span(rows)
    split = end

    def emit(layer, pair, both):
        margin = RIM - 1 - layer
        for q in range(2):
            r = 2 * pair + q
            value = both[:, q * lanes : (q + 1) * lanes]
            if layer == 0:
                value = jnp.maximum(value, 0.1 * value)
            elif layer % 2 == 1:
                value = jnp.maximum(value, 0.0)
            else:
                value = value + layers[layer - 2][r + 2, 0].astype(F32)
            if r < margin:
                value = jnp.where(place.above, value, 0.0)
            elif r >= margin + rows:
                value = jnp.where(place.below, value, 0.0)
            if layer < 2 * RES_BLOCKS:
                put(layers[layer], (r,), value, low, sub)
            else:
                if sends:
                    latest[r] = value.astype(BF16)
                else:
                    plain_rows[r] = value

    fetches = [operand(part) for part in range(parts)]
    join = tuple(range(parts))
    for begin, stop in ((0, first), (first, end), (end, count)):
        made = None
        if begin != first:
            made = two_row_conv(fetches, begin, stop - begin, w_ref, join)
        for k in range(begin, stop):
            if begin == first:
                at = k - first if tick == 0 else k
                both = acc_in[at * pairs : (at + 1) * pairs]
            else:
                both = made[(k - begin) * pairs : (k - begin + 1) * pairs]
                if tick > 0:
                    both = both + acc_in[k * pairs : (k + 1) * pairs]
            emit(0, k, both)
    for layer in range(1, 2 * RES_BLOCKS + 1):
        count -= 1
        split -= 1
        for begin, stop in ((0, split), (split, count)):
            made = two_row_conv(
                [lambda r, h: layers[layer - 1][r, h]], begin, stop - begin, w_ref, (2 + layer,)
            )
            for k in range(begin, stop):
                emit(layer, k, made[(k - begin) * pairs : (k - begin + 1) * pairs])
    if not sends:
        rows_to_natural(natural, plain_rows)
        return
    send_one, send_two = sends

    @pl.when(even)
    def _():
        send_one[...] = latest[rows - RIM : rows]
        send_two[...] = latest[0:RIM]

    @pl.when(jnp.logical_not(even))
    def _():
        send_one[...] = latest[0:RIM]
        send_two[...] = latest[rows - RIM : rows]


def pair_weights(weight):
    before, here, after = weight[:, :, 0], weight[:, :, 1], weight[:, :, 2]
    zero = jnp.zeros_like(here)
    return jnp.concatenate(
        [
            jnp.concatenate([here, before], axis=-1),
            jnp.concatenate([after, here], axis=-1),
            jnp.concatenate([zero, after], axis=-1),
            jnp.concatenate([before, zero], axis=-1),
        ],
        axis=2,
    )


def all_weights(join_weight, res_weight, channels):
    return jnp.concatenate(
        [
            pair_weights(
                join_weight.reshape(3, 3, 3, channels, channels).transpose(2, 0, 1, 3, 4)
            ),
            pair_weights(res_weight.reshape(2 * RES_BLOCKS, 3, 3, channels, channels)),
        ],
        axis=0,
    )


def shards(features, carried, flow_shift, clip_start, join_weight, res_weight):
    rows = features.shape[1]
    wide = features.shape[2]
    channels = join_weight.shape[2]
    lanes = 2 * channels
    pairs = wide // lanes
    slots = lax.axis_size("rows")
    bands = slots // SECTIONS
    lead = bands // 2
    index = lax.axis_index("rows")
    even = (index + (slots - lead)) % 2 == 0
    index = index.astype(jnp.int32).reshape(1)

    def route(move):
        return [(i, move(i) % slots) for i in range(slots)]

    def is_even(i):
        return (i - lead) % 2 == 0

    swap_one = route(lambda i: i + 1 if is_even(i) else i - 1)
    swap_two = route(lambda i: i - 1 if is_even(i) else i + 1)

    def shift_by(count):
        return route(lambda i: i + count)

    def send(block, path):
        return lax.ppermute(block, "rows", path)

    flow = jnp.transpose(flow_shift, (1, 2, 0))
    made = rows + 2 * (RIM - 1)
    total = made // 2 * pairs
    span = rows + 2 * RIM
    long = pairs + 2 * PAD
    first, end = local_span(rows)
    params = pltpu.CompilerParams(vmem_limit_bytes=GRANT)

    def cost(pairs_done, depth):
        return pl.CostEstimate(
            flops=pairs_done * pairs * depth * 16 * lanes * lanes,
            bytes_accessed=4 << 20,
            transcendentals=0,
        )

    def operands(*lead_shape):
        return lead_shape + (2, pairs, lanes)

    def pack():
        def kernel(*refs):
            pack_kernel(slots, *refs)

        halo = jax.ShapeDtypeStruct((3 * RIM + 1, pairs, lanes), BF16)
        return pl.pallas_call(
            kernel,
            out_shape=(jax.ShapeDtypeStruct((3, rows, pairs, lanes), BF16), halo, halo),
            in_specs=[SMEM, HBM, HBM, HBM],
            out_specs=(VMEM, VMEM, VMEM),
            scratch_shapes=[
                pltpu.VMEM((3, rows, wide), BF16),
                pltpu.VMEM((3, rows * (pairs + SUB), lanes), F32),
                pltpu.SemaphoreType.DMA((4,)),
                pltpu.SMEM(flow.shape, jnp.int32),
            ],
            compiler_params=params,
            name="pack",
        )(index, in_hbm(flow), in_hbm(carried), in_hbm(features))

    def frames(features):
        later = TICKS - 1
        frame = jax.ShapeDtypeStruct((rows + 2, pairs, lanes), BF16)
        return pl.pallas_call(
            frame_kernel,
            out_shape=(frame,) * later,
            in_specs=[HBM, HBM],
            out_specs=(VMEM,) * later,
            scratch_shapes=[
                pltpu.VMEM((later, rows, wide), BF16),
                pltpu.VMEM((later, rows * (pairs + SUB), lanes), F32),
                pltpu.SemaphoreType.DMA((later + 1,)),
                pltpu.SMEM(flow.shape, jnp.int32),
            ],
            compiler_params=params,
            name="frame",
        )(in_hbm(flow), in_hbm(features))

    def start(own):
        def kernel(*refs):
            start_kernel(slots, *refs)

        return pl.pallas_call(
            kernel,
            out_shape=(
                jax.ShapeDtypeStruct(((end - first) * pairs, 2 * lanes), F32),
                jax.ShapeDtypeStruct(operands(3, rows), BF16),
            ),
            in_specs=[SMEM, SMEM, SMEM, VMEM, VMEM],
            out_specs=(VMEM, VMEM),
            scratch_shapes=[pltpu.VMEM((3 * rows, long, lanes), F32)],
            compiler_params=params,
            cost_estimate=cost(end - first, 3),
            name="start",
        )(index, clip_start, flow, own, weights)

    def ahead(tick, latest, prev, prev_one, prev_two, feats):
        def kernel(*refs):
            ahead_kernel(slots, tick, tick > 1, *refs)

        whole = (TICKS,) if tick == 1 else ()
        return pl.pallas_call(
            kernel,
            out_shape=(
                jax.ShapeDtypeStruct((total, 2 * lanes), F32),
                jax.ShapeDtypeStruct(operands(1, rows), BF16),
                jax.ShapeDtypeStruct((2,), jnp.int32),
                jax.ShapeDtypeStruct(whole + (rows, wide), BF16),
            ),
            in_specs=[SMEM, SMEM] + [VMEM] * 8,
            out_specs=(VMEM, VMEM, SMEM, HBM if whole else VMEM),
            scratch_shapes=[
                pltpu.VMEM((2 * span, long, lanes), F32),
                pltpu.VMEM((rows, long, lanes), F32),
                pltpu.VMEM(operands(2, span), BF16),
                pltpu.VMEM((rows, pairs, lanes), F32),
            ]
            + ([pltpu.VMEM((rows, wide), BF16), pltpu.SemaphoreType.DMA] if whole else []),
            compiler_params=params,
            cost_estimate=cost(made, 1),
        )(index, clip_start, latest, prev, prev_one, prev_two, *feats, weights)

    def finish(tick, shifts, acc, ops, one, two):
        last = tick + 1 == TICKS
        parts = ops.shape[0]

        def kernel(index, clip, shifts, acc_in, ops, one, two, w_ref, *rest):
            if last:
                natural, *scratch = rest
                latest, sends = None, ()
            else:
                latest, send_one, send_two, *scratch = rest
                natural, sends = None, (send_one, send_two)
            window, *layers, padded, plain_rows = scratch
            finish_kernel(
                slots, tick, index, clip, shifts, acc_in, ops, one, two, w_ref,
                latest, natural, sends, window, layers, padded, plain_rows,
            )

        halo = jax.ShapeDtypeStruct((RIM, pairs, lanes), BF16)
        if last:
            outs = (jax.ShapeDtypeStruct((rows, wide), BF16),)
        else:
            outs = (jax.ShapeDtypeStruct((rows, pairs, lanes), BF16), halo, halo)
        return pl.pallas_call(
            kernel,
            out_shape=outs,
            in_specs=[SMEM, SMEM, SMEM] + [VMEM] * 5,
            out_specs=(VMEM,) * len(outs),
            scratch_shapes=[pltpu.VMEM(operands(parts, 2 * RIM), BF16)]
            + [pltpu.VMEM(operands(made - 2 * layer), BF16) for layer in range(2 * RES_BLOCKS)]
            + [
                pltpu.VMEM((parts * 2 * RIM, long, lanes), F32),
                pltpu.VMEM((rows, pairs, lanes), F32),
            ],
            compiler_params=params,
            cost_estimate=cost(made + made // 2 * parts, 1),
        )(index, clip_start, shifts, acc, ops, one, two, weights)

    own, first_one, first_two = pack()
    later_features, first_one, first_two = lax.optimization_barrier(
        (features, first_one, first_two)
    )
    halo_two = send(first_two, swap_two)
    halo_one = send(first_one, swap_one)
    framed = frames(later_features)
    framed, own, join_weight, res_weight = lax.optimization_barrier(
        (framed, own, join_weight, res_weight)
    )
    feats = [[] for _ in range(TICKS)]
    for tick in range(1, TICKS):
        frame = framed[tick - 1]
        back = -bands * tick
        feats[tick].append(send(frame, shift_by(back)))
        if tick == 1:
            feats[tick].append(send(frame[rows + 1 - RIM :], shift_by(back + 1)))
            feats[tick].append(send(frame[: RIM + 1], shift_by(back - 1)))
    weights = all_weights(join_weight, res_weight, channels)
    acc, ops = start(own)
    latest, send_one, send_two = finish(
        0, jnp.zeros((2,), jnp.int32), acc, ops, halo_one, halo_two
    )
    prev, prev_one, prev_two = own[0], halo_one, halo_two
    for tick in range(1, TICKS):
        two = send(send_two, swap_two)
        one = send(send_one, swap_one)
        acc, ops, shifts, natural = ahead(tick, latest, prev, prev_one, prev_two, feats[tick])
        if tick == 1:
            result = natural
        else:
            moved = send(natural, shift_by(bands * (tick - 1)))
            result = lax.dynamic_update_slice_in_dim(result, moved[None], tick - 1, 0)
        if tick + 1 < TICKS:
            acc, frame = lax.optimization_barrier((acc, feats[tick + 1][0]))
            begin_one = jnp.where(even, rows + 1 - RIM, 0)
            begin_two = jnp.where(even, 0, rows + 1 - RIM)
            size = RIM + 1
            part_two = lax.dynamic_slice_in_dim(frame, begin_two, size, axis=0)
            part_one = lax.dynamic_slice_in_dim(frame, begin_one, size, axis=0)
            frame_two = send(part_two, swap_two)
            frame_one = send(part_one, swap_one)
            feats[tick + 1] = [
                frame,
                jnp.where(even, frame_two, frame_one),
                jnp.where(even, frame_one, frame_two),
            ]
        prev, prev_one, prev_two = latest, one, two
        outs = finish(tick, shifts, acc, ops, one, two)
        if tick + 1 < TICKS:
            latest, send_one, send_two = outs
    moved = send(outs[0], shift_by(bands * (TICKS - 1)))
    return lax.dynamic_update_slice_in_dim(result, moved[None], TICKS - 1, 0)


def solution(mesh):
    in_specs = (
        P(None, ("groups", "rows"), None),
        P(None, ("groups", "rows"), None),
        P(None, ("groups", "rows"), None),
        P("groups"),
        P(),
        P(),
    )
    out_specs = P(None, ("groups", "rows"), None)

    return jax.shard_map(shards, mesh=mesh, in_specs=in_specs, out_specs=out_specs, check_vma=False)
```

```python
import jax
import jax.numpy as jnp
from jax import lax
from jax.experimental import pallas as pl
from jax.experimental.pallas import tpu as pltpu
from jax.sharding import PartitionSpec as P


TICKS = 3
SECTIONS = 4
RES_BLOCKS = 2
RIM = 1 + 2 * RES_BLOCKS
PAD = 8
SUB = 8
GRANT = 24 << 20

BF16 = jnp.bfloat16
F32 = jnp.float32
VMEM = pl.BlockSpec(memory_space=pltpu.VMEM)
SMEM = pl.BlockSpec(memory_space=pltpu.SMEM)
HBM = pl.BlockSpec(memory_space=pltpu.HBM)


def in_hbm(block):
    return pltpu.with_memory_space_constraint(block, pltpu.HBM)


def lane_low(lanes):
    return lax.broadcasted_iota(jnp.int32, (SUB, lanes), 1) < lanes // 2


def sublane(lanes):
    return lax.broadcasted_iota(jnp.int32, (SUB, lanes), 0)


def store_operand(dst, index, groups, low):
    here = jnp.concatenate(groups[1:-1], axis=0)
    beside = jnp.concatenate(
        [jnp.where(low, groups[v + 2], groups[v]) for v in range(len(groups) - 2)], axis=0
    )
    dst[index + (0,)] = here.astype(BF16)
    dst[index + (1,)] = beside.astype(BF16)


def put(dst, index, row, low, sub):
    count = row.shape[0] // SUB
    groups = [row[SUB * v : SUB * v + SUB] for v in range(count)]
    before = jnp.where(sub > 0, pltpu.roll(groups[-1], 1, 0), 0.0)
    after = jnp.where(sub < SUB - 1, pltpu.roll(groups[0], SUB - 1, 0), 0.0)
    store_operand(dst, index, [before] + groups + [after], low)


def stage(padded, row, value, interleaved):
    pairs = value.shape[0]
    count = pairs // SUB
    if interleaved:
        for v in range(count):
            padded[row, pl.ds(PAD + v, SUB, stride=count), :] = value[SUB * v : SUB * v + SUB]
    else:
        padded[row, PAD : PAD + pairs, :] = value


def put_plain(dst, index, padded, row, low):
    count = (padded.shape[1] - 2 * PAD) // SUB
    groups = [
        padded[row, pl.ds(PAD + v, SUB, stride=count), :] for v in range(-1, count + 1)
    ]
    store_operand(dst, index, groups, low)


def put_warped(dst, index, padded, row, shift, low, sub):
    count = (padded.shape[1] - 2 * PAD) // SUB
    lanes = padded.shape[2]
    start = PAD - (shift >> 1)
    is_odd = (shift & 1) == 1
    raw = [
        padded[row, pl.ds(start + v, SUB, stride=count), :] for v in range(-2, count + 1)
    ]
    groups = []
    for v in range(1, len(raw)):
        odd = pltpu.roll(jnp.where(low, raw[v], raw[v - 1]), lanes // 2, 1)
        groups.append(jnp.where(is_odd, odd, raw[v]))
    groups[0] = jnp.where(sub > 0, groups[0], 0.0)
    groups[-1] = jnp.where(sub < SUB - 1, groups[-1], 0.0)
    store_operand(dst, index, groups, low)


def two_row_weight(w_ref, layers):
    zero = jnp.zeros(w_ref.shape[2:], BF16)
    upper, lower = [], []
    for layer in layers:
        w = [w_ref[layer, a] for a in range(3)]
        upper += w + [zero]
        lower += [zero] + w
    return jnp.concatenate(
        [jnp.concatenate(upper, axis=1), jnp.concatenate(lower, axis=1)], axis=0
    )


def two_row_conv(fetches, first, count, w_ref, layers):
    columns = []
    for fetch in fetches:
        for i in range(4):
            for part in range(2):
                columns.append(
                    jnp.concatenate(
                        [fetch(2 * (first + k) + i, part) for k in range(count)], axis=0
                    )
                )
    return lax.dot_general(
        jnp.concatenate(columns, axis=1),
        two_row_weight(w_ref, layers),
        (((1,), (1,)), ((), ())),
        preferred_element_type=F32,
    )


def scalars_of(row):
    half = row.shape[0] // 2
    wide = row.astype(F32)
    return (
        jnp.max(wide[0:SUB]).astype(jnp.int32),
        jnp.max(wide[half : half + SUB]).astype(jnp.int32),
    )


def local_span(band_rows):
    return (RIM + 1) // 2, (RIM + band_rows - 4) // 2 + 1


def clear_pads(padded):
    rows, long, lanes = padded.shape
    for row in range(rows):
        padded[row, 0:PAD, :] = jnp.zeros((PAD, lanes), F32)
        padded[row, long - PAD :, :] = jnp.zeros((PAD, lanes), F32)


class Place:
    def __init__(self, index, clip, slots):
        bands = slots // SECTIONS
        position = lax.rem(index[0] + (slots - bands // 2), slots)
        self.band = lax.rem(position, bands)
        self.owner = lax.div(position, bands)
        self.clip = clip
        self.even = lax.rem(self.band, 2) == 0
        self.above = self.band > 0
        self.below = self.band < bands - 1

    def keep(self, tick):
        return self.clip[lax.rem(self.owner + tick, SECTIONS)] != tick


def natural_to_rows(scratch, block):
    rows = block.shape[0]
    lanes = scratch.shape[1]
    pairs = block.shape[1] // lanes
    pitch = scratch.shape[0] // rows
    for p in range(pairs):
        tile = block[:, p * lanes : (p + 1) * lanes].astype(F32)
        scratch[pl.ds(p, rows, stride=pitch), :] = tile
    return [scratch[r * pitch : r * pitch + pairs, :].astype(BF16) for r in range(rows)]


def shift_row(flow, tick, pairs, lanes):
    halves = [
        jnp.full((pairs // 2, lanes), flow[0, which, tick].astype(F32)) for which in range(2)
    ]
    return jnp.concatenate(halves, axis=0).astype(BF16)


def pack_kernel(
    slots, index, flow_in, carried, features, own, first_one, first_two, natural, scratch, sems,
    flow,
):
    _, rows, pairs, lanes = own.shape
    place = Place(index, None, slots)
    copies = [
        pltpu.make_async_copy(block, natural.at[part], sems.at[part])
        for part, block in enumerate((carried.at[0], carried.at[1], features.at[0]))
    ]
    copies.append(pltpu.make_async_copy(flow_in, flow, sems.at[3]))
    for copy in copies:
        copy.start()
    for part in range(3):
        copies[part].wait()
        for r, row in enumerate(natural_to_rows(scratch.at[part], natural.at[part])):
            own[part, r] = row
    copies[3].wait()
    mark = shift_row(flow, 0, pairs, lanes)
    first_one[3 * RIM] = mark
    first_two[3 * RIM] = mark
    for last, first, chosen in (
        (first_one, first_two, place.even),
        (first_two, first_one, jnp.logical_not(place.even)),
    ):

        @pl.when(chosen)
        def _():
            for part in range(3):
                last[part * RIM : (part + 1) * RIM] = own[part, rows - RIM : rows]
                first[part * RIM : (part + 1) * RIM] = own[part, 0:RIM]


def frame_kernel(flow_in, features, *rest):
    *framed, natural, scratch, sems, flow = rest
    _, pairs, lanes = framed[0].shape
    rows = framed[0].shape[0] - 2
    copies = [
        pltpu.make_async_copy(features.at[later + 1], natural.at[later], sems.at[later])
        for later in range(len(framed))
    ]
    copies.append(pltpu.make_async_copy(flow_in, flow, sems.at[len(framed)]))
    for copy in copies:
        copy.start()
    for later, frame in enumerate(framed):
        copies[later].wait()
        for r, row in enumerate(natural_to_rows(scratch.at[later], natural.at[later])):
            frame[1 + r] = row
    copies[-1].wait()
    for later, frame in enumerate(framed):
        mark = shift_row(flow, later + 1, pairs, lanes)
        frame[0] = mark
        frame[rows + 1] = mark


def own_terms(sources, w_ref, acc, ops, padded, low, sub):
    rows = ops.shape[1]
    at = 0
    for part, (row, shift, interleaved) in enumerate(sources):
        for r in range(rows):
            stage(padded, at, row(r), interleaved)
            if shift is None:
                put_plain(ops, (part, r), padded, at, low)
            else:
                put_warped(ops, (part, r), padded, at, shift, low, sub)
            at += 1
    first, end = local_span(rows)
    fetches = [lambda r, h, part=part: ops[part, r - RIM, h] for part in range(3)]
    acc[...] = two_row_conv(fetches, first, end - first, w_ref, (0, 1, 2))


def start_kernel(slots, index, clip, flow, own, w_ref, acc, ops, padded):
    lanes = own.shape[3]
    keep = Place(index, clip, slots).keep(0)
    clear_pads(padded)

    def kept(part):
        return lambda r: jnp.where(keep, own[part, r].astype(F32), 0.0)

    own_terms(
        (
            (kept(0), flow[0, 0, 0], False),
            (kept(1), flow[0, 1, 0], False),
            (lambda r: own[2, r].astype(F32), None, False),
        ),
        w_ref, acc, ops, padded, lane_low(lanes), sublane(lanes),
    )


def ahead_kernel(
    slots, tick, index, clip, latest, prev, feat, w_ref, acc, ops, natural, padded, plain_rows,
    *copying,
):
    rows, _, lanes = latest.shape
    place = Place(index, clip, slots)
    keep_latest = place.keep(tick)
    keep_earlier = keep_latest & place.keep(tick - 1)
    shift = scalars_of(feat[0])
    clear_pads(padded)
    for r in range(rows):
        plain_rows[r] = latest[r].astype(F32)
    own_terms(
        (
            (lambda r: jnp.where(keep_latest, plain_rows[r], 0.0), shift[0], True),
            (lambda r: jnp.where(keep_earlier, prev[r].astype(F32), 0.0), shift[1], tick > 1),
            (lambda r: feat[1 + r].astype(F32), None, False),
        ),
        w_ref, acc, ops, padded, lane_low(lanes), sublane(lanes),
    )
    if copying:
        natural_rows, sem = copying
        rows_to_natural(natural_rows, plain_rows)
        copy = pltpu.make_async_copy(natural_rows, natural.at[0], sem)
        copy.start()
        copy.wait()
    else:
        rows_to_natural(natural, plain_rows)


def rows_to_natural(natural, plain_rows):
    rows, pairs, lanes = plain_rows.shape
    groups = pairs // SUB
    flat = plain_rows.reshape(rows * pairs, lanes)
    for v in range(groups):
        for s in range(SUB):
            pair = groups * s + v
            tile = flat[pl.ds(SUB * v + s, rows, stride=pairs), :]
            natural[:, pair * lanes : (pair + 1) * lanes] = tile.astype(BF16)


def finish_kernel(
    slots, tick, index, clip, acc_in, ops, halo_one, halo_two, prev, w_ref,
    latest, natural, sends, window, layers, padded, plain_rows,
):
    parts, rows, _, pairs, lanes = ops.shape
    place = Place(index, clip, slots)
    even = place.even
    low, sub = lane_low(lanes), sublane(lanes)
    keep = place.keep(tick)
    keep_both = keep if tick == 0 else keep & place.keep(tick - 1)

    def above(r, one=halo_one, two=halo_two):
        return jnp.where(even, two[r], one[r])

    def below(r, one=halo_one, two=halo_two):
        return jnp.where(even, one[r], two[r])

    if tick == 0:
        marks = 3 * RIM
        sides = [
            (side, [lambda r, k=k, side=side: side(k * RIM + r) for k in range(3)],
             scalars_of(side(marks)))
            for side in (above, below)
        ]
    else:
        sides = [
            (
                side,
                [
                    lambda r, side=side: side(r),
                    lambda r, side=side: side(r, *prev),
                    lambda r, side=side, skip=skip: side(RIM + skip + r),
                ],
                scalars_of(side(mark)),
            )
            for side, skip, mark in ((above, 0, 2 * RIM), (below, 1, RIM))
        ]
    clear_pads(padded)
    at = 0
    for which, (side, sources, shift) in enumerate(sides):
        inside = place.above if which == 0 else place.below
        for r in range(RIM):
            for part in range(parts):
                row = sources[part](r).astype(F32)
                ok = inside & (keep, keep_both)[part] if part < 2 else inside
                interleaved = tick > part and part < 2
                stage(padded, at, jnp.where(ok, row, 0.0), interleaved)
                slot = which * RIM + r
                if part < 2:
                    put_warped(window, (part, slot), padded, at, shift[part], low, sub)
                else:
                    put_plain(window, (part, slot), padded, at, low)
                at += 1

    def operand(part):
        def fetch(r, h):
            if r < RIM:
                return window[part, r, h]
            if r < RIM + rows:
                return ops[part, r - RIM, h]
            return window[part, r - rows, h]

        return fetch

    count = (rows + 2 * RIM - 2) // 2
    first, end = local_span(rows)
    split = end

    def emit(layer, pair, both):
        margin = RIM - 1 - layer
        for q in range(2):
            r = 2 * pair + q
            value = both[:, q * lanes : (q + 1) * lanes]
            if layer == 0:
                value = jnp.maximum(value, 0.1 * value)
            elif layer % 2 == 1:
                value = jnp.maximum(value, 0.0)
            else:
                value = value + layers[layer - 2][r + 2, 0].astype(F32)
            if r < margin:
                value = jnp.where(place.above, value, 0.0)
            elif r >= margin + rows:
                value = jnp.where(place.below, value, 0.0)
            if layer < 2 * RES_BLOCKS:
                put(layers[layer], (r,), value, low, sub)
            else:
                if sends:
                    latest[r] = value.astype(BF16)
                else:
                    plain_rows[r] = value

    fetches = [operand(part) for part in range(parts)]
    join = tuple(range(parts))
    for begin, stop in ((0, first), (first, end), (end, count)):
        made = None
        if begin != first:
            made = two_row_conv(fetches, begin, stop - begin, w_ref, join)
        for k in range(begin, stop):
            source = acc_in if begin == first else made
            emit(0, k, source[(k - begin) * pairs : (k - begin + 1) * pairs])
    for layer in range(1, 2 * RES_BLOCKS + 1):
        count -= 1
        split -= 1
        for begin, stop in ((0, split), (split, count)):
            made = two_row_conv(
                [lambda r, h: layers[layer - 1][r, h]], begin, stop - begin, w_ref, (2 + layer,)
            )
            for k in range(begin, stop):
                emit(layer, k, made[(k - begin) * pairs : (k - begin + 1) * pairs])
    if not sends:
        rows_to_natural(natural, plain_rows)
        return
    send_one, send_two = sends

    @pl.when(even)
    def _():
        send_one[...] = latest[rows - RIM : rows]
        send_two[...] = latest[0:RIM]

    @pl.when(jnp.logical_not(even))
    def _():
        send_one[...] = latest[0:RIM]
        send_two[...] = latest[rows - RIM : rows]


def weight_kernel(join, res, w_ref):
    channels = join.shape[1]
    zero = jnp.zeros((channels, channels), F32)

    def fill(layer, a, taps):
        before, here, after = taps
        w_ref[layer, a, 0:channels] = jnp.concatenate([here, after, zero, before], axis=1).astype(
            BF16
        )
        w_ref[layer, a, channels : 2 * channels] = jnp.concatenate(
            [before, here, after, zero], axis=1
        ).astype(BF16)

    for a in range(3):
        whole = join[a].astype(F32)
        for part in range(3):
            starts = [(3 * b + part) * channels for b in range(3)]
            fill(part, a, [whole[:, at : at + channels] for at in starts])
    for layer in range(res.shape[0]):
        for a in range(3):
            whole = res[layer, a].astype(F32)
            fill(3 + layer, a, [whole[:, b * channels : (b + 1) * channels] for b in range(3)])


def shards(features, carried, flow_shift, clip_start, join_weight, res_weight):
    rows = features.shape[1]
    wide = features.shape[2]
    channels = join_weight.shape[2]
    lanes = 2 * channels
    pairs = wide // lanes
    slots = lax.axis_size("rows")
    bands = slots // SECTIONS
    lead = bands // 2
    index = lax.axis_index("rows")
    even = (index + (slots - lead)) % 2 == 0
    index = index.astype(jnp.int32).reshape(1)

    def route(move):
        return [(i, move(i) % slots) for i in range(slots)]

    def is_even(i):
        return (i - lead) % 2 == 0

    swap_one = route(lambda i: i + 1 if is_even(i) else i - 1)
    swap_two = route(lambda i: i - 1 if is_even(i) else i + 1)

    def shift_by(count):
        return route(lambda i: i + count)

    def send(block, path):
        return lax.ppermute(block, "rows", path)

    flow = jnp.transpose(flow_shift, (1, 2, 0))
    made = rows + 2 * (RIM - 1)
    long = pairs + 2 * PAD
    first, end = local_span(rows)
    params = pltpu.CompilerParams(vmem_limit_bytes=GRANT)

    def cost(pairs_done, depth):
        return pl.CostEstimate(
            flops=pairs_done * pairs * depth * 16 * lanes * lanes,
            bytes_accessed=4 << 20,
            transcendentals=0,
        )

    def operands(*lead_shape):
        return lead_shape + (2, pairs, lanes)

    def pack():
        def kernel(*refs):
            pack_kernel(slots, *refs)

        halo = jax.ShapeDtypeStruct((3 * RIM + 1, pairs, lanes), BF16)
        return pl.pallas_call(
            kernel,
            out_shape=(jax.ShapeDtypeStruct((3, rows, pairs, lanes), BF16), halo, halo),
            in_specs=[SMEM, HBM, HBM, HBM],
            out_specs=(VMEM, VMEM, VMEM),
            scratch_shapes=[
                pltpu.VMEM((3, rows, wide), BF16),
                pltpu.VMEM((3, rows * (pairs + SUB), lanes), F32),
                pltpu.SemaphoreType.DMA((4,)),
                pltpu.SMEM(flow.shape, jnp.int32),
            ],
            compiler_params=params,
            name="pack",
        )(index, in_hbm(flow), in_hbm(carried), in_hbm(features))

    def frames(features):
        later = TICKS - 1
        frame = jax.ShapeDtypeStruct((rows + 2, pairs, lanes), BF16)
        return pl.pallas_call(
            frame_kernel,
            out_shape=(frame,) * later,
            in_specs=[HBM, HBM],
            out_specs=(VMEM,) * later,
            scratch_shapes=[
                pltpu.VMEM((later, rows, wide), BF16),
                pltpu.VMEM((later, rows * (pairs + SUB), lanes), F32),
                pltpu.SemaphoreType.DMA((later + 1,)),
                pltpu.SMEM(flow.shape, jnp.int32),
            ],
            compiler_params=params,
            name="frame",
        )(in_hbm(flow), in_hbm(features))

    def start(own):
        def kernel(*refs):
            start_kernel(slots, *refs)

        return pl.pallas_call(
            kernel,
            out_shape=(
                jax.ShapeDtypeStruct(((end - first) * pairs, 2 * lanes), F32),
                jax.ShapeDtypeStruct(operands(3, rows), BF16),
            ),
            in_specs=[SMEM, SMEM, SMEM, VMEM, VMEM],
            out_specs=(VMEM, VMEM),
            scratch_shapes=[pltpu.VMEM((3 * rows, long, lanes), F32)],
            compiler_params=params,
            cost_estimate=cost(end - first, 3),
            name="start",
        )(index, clip_start, flow, own, weights)

    def ahead(tick, latest, prev, feat):
        def kernel(*refs):
            ahead_kernel(slots, tick, *refs)

        whole = (TICKS,) if tick == 1 else ()
        return pl.pallas_call(
            kernel,
            out_shape=(
                jax.ShapeDtypeStruct(((end - first) * pairs, 2 * lanes), F32),
                jax.ShapeDtypeStruct(operands(3, rows), BF16),
                jax.ShapeDtypeStruct(whole + (rows, wide), BF16),
            ),
            in_specs=[SMEM, SMEM] + [VMEM] * 4,
            out_specs=(VMEM, VMEM, HBM if whole else VMEM),
            scratch_shapes=[
                pltpu.VMEM((3 * rows, long, lanes), F32),
                pltpu.VMEM((rows, pairs, lanes), F32),
            ]
            + ([pltpu.VMEM((rows, wide), BF16), pltpu.SemaphoreType.DMA] if whole else []),
            compiler_params=params,
            cost_estimate=cost(end - first, 3),
        )(index, clip_start, latest, prev, feat, weights)

    def finish(tick, acc, ops, one, two, prev=()):
        last = tick + 1 == TICKS
        parts = ops.shape[0]

        def kernel(index, clip, acc_in, ops, one, two, *rest):
            before, (w_ref, *rest) = rest[: len(prev)], rest[len(prev) :]
            if last:
                natural, *scratch = rest
                latest, sends = None, ()
            else:
                latest, send_one, send_two, *scratch = rest
                natural, sends = None, (send_one, send_two)
            window, *layers, padded, plain_rows = scratch
            finish_kernel(
                slots, tick, index, clip, acc_in, ops, one, two, before, w_ref,
                latest, natural, sends, window, layers, padded, plain_rows,
            )

        halo = jax.ShapeDtypeStruct((RIM, pairs, lanes), BF16)
        if last:
            outs = (jax.ShapeDtypeStruct((rows, wide), BF16),)
        else:
            outs = (jax.ShapeDtypeStruct((rows, pairs, lanes), BF16), halo, halo)
        return pl.pallas_call(
            kernel,
            out_shape=outs,
            in_specs=[SMEM, SMEM] + [VMEM] * (5 + len(prev)),
            out_specs=(VMEM,) * len(outs),
            scratch_shapes=[pltpu.VMEM(operands(parts, 2 * RIM), BF16)]
            + [pltpu.VMEM(operands(made - 2 * layer), BF16) for layer in range(2 * RES_BLOCKS)]
            + [
                pltpu.VMEM((parts * 2 * RIM, long, lanes), F32),
                pltpu.VMEM((rows, pairs, lanes), F32),
            ],
            compiler_params=params,
            cost_estimate=cost(made + made // 2 * parts, 1),
        )(index, clip_start, acc, ops, one, two, *prev, weights)

    own, first_one, first_two = pack()
    later_features, first_one, first_two = lax.optimization_barrier(
        (features, first_one, first_two)
    )
    halo_two = send(first_two, swap_two)
    halo_one = send(first_one, swap_one)
    framed = frames(later_features)
    framed, own, join_weight, res_weight = lax.optimization_barrier(
        (framed, own, join_weight, res_weight)
    )

    def bring(tick):
        return send(framed[tick - 1], shift_by(-bands * tick))

    feat = bring(1)
    weights = pl.pallas_call(
        weight_kernel,
        out_shape=jax.ShapeDtypeStruct((3 + 2 * RES_BLOCKS, 3, lanes, 2 * lanes), BF16),
        in_specs=[VMEM, VMEM],
        out_specs=VMEM,
        compiler_params=params,
        name="weights",
    )(jnp.transpose(join_weight, (0, 2, 1)), jnp.transpose(res_weight, (0, 1, 3, 2)))
    acc, ops = start(own)
    begin_one = jnp.where(even, rows + 1 - RIM, 0)
    begin_two = jnp.where(even, 0, rows + 1 - RIM)

    def with_rim(block, frame, begin):
        return jnp.concatenate(
            [block, lax.dynamic_slice_in_dim(frame, begin, RIM + 1, axis=0)], axis=0
        )

    one, two = halo_one, halo_two
    prev = own[0]
    outs = finish(0, acc, ops, one, two)
    for tick in range(1, TICKS):
        latest, send_one, send_two = outs
        feat, latest, send_one, send_two = lax.optimization_barrier(
            (feat, latest, send_one, send_two)
        )
        before = one, two
        two = send(with_rim(send_two, feat, begin_two), swap_two)
        one = send(with_rim(send_one, feat, begin_one), swap_one)
        if tick + 1 < TICKS:
            next_feat = bring(tick + 1)
        acc, ops, natural = ahead(tick, latest, prev, feat)
        if tick == 1:
            result = natural
        else:
            moved = send(natural, shift_by(bands * (tick - 1)))
            result = lax.dynamic_update_slice_in_dim(result, moved[None], tick - 1, 0)
        prev = latest
        feat = next_feat
        outs = finish(tick, acc, ops, one, two, before)
    moved = send(outs[0], shift_by(bands * (TICKS - 1)))
    return lax.dynamic_update_slice_in_dim(result, moved[None], TICKS - 1, 0)


def solution(mesh):
    in_specs = (
        P(None, ("groups", "rows"), None),
        P(None, ("groups", "rows"), None),
        P(None, ("groups", "rows"), None),
        P("groups"),
        P(),
        P(),
    )
    out_specs = P(None, ("groups", "rows"), None)

    return jax.shard_map(
        shards, mesh=mesh, in_specs=in_specs, out_specs=out_specs, check_vma=False
    )
```

```python
import jax
import jax.numpy as jnp
from jax import lax
from jax.experimental import pallas as pl
from jax.experimental.pallas import tpu as pltpu
from jax.sharding import PartitionSpec as P


TICKS = 3
SECTIONS = 4
RES_BLOCKS = 2
RIM = 1 + 2 * RES_BLOCKS
PAD = 8
SUB = 8
GRANT = 24 << 20

BF16 = jnp.bfloat16
F32 = jnp.float32
VMEM = pl.BlockSpec(memory_space=pltpu.VMEM)
SMEM = pl.BlockSpec(memory_space=pltpu.SMEM)
HBM = pl.BlockSpec(memory_space=pltpu.HBM)


def in_hbm(block):
    return pltpu.with_memory_space_constraint(block, pltpu.HBM)


def lane_low(lanes):
    return lax.broadcasted_iota(jnp.int32, (SUB, lanes), 1) < lanes // 2


def sublane(lanes):
    return lax.broadcasted_iota(jnp.int32, (SUB, lanes), 0)


def store_operand(dst, index, groups, low):
    here = jnp.concatenate(groups[1:-1], axis=0)
    beside = jnp.concatenate(
        [jnp.where(low, groups[v + 2], groups[v]) for v in range(len(groups) - 2)], axis=0
    )
    dst[index + (0,)] = here.astype(BF16)
    dst[index + (1,)] = beside.astype(BF16)


def put(dst, index, row, low, sub):
    count = row.shape[0] // SUB
    groups = [row[SUB * v : SUB * v + SUB] for v in range(count)]
    before = jnp.where(sub > 0, pltpu.roll(groups[-1], 1, 0), 0.0)
    after = jnp.where(sub < SUB - 1, pltpu.roll(groups[0], SUB - 1, 0), 0.0)
    store_operand(dst, index, [before] + groups + [after], low)


def stage(padded, row, value, interleaved):
    pairs = value.shape[0]
    count = pairs // SUB
    if interleaved:
        for v in range(count):
            padded[row, pl.ds(PAD + v, SUB, stride=count), :] = value[SUB * v : SUB * v + SUB]
    else:
        padded[row, PAD : PAD + pairs, :] = value


def put_plain(dst, index, padded, row, low):
    count = (padded.shape[1] - 2 * PAD) // SUB
    groups = [
        padded[row, pl.ds(PAD + v, SUB, stride=count), :] for v in range(-1, count + 1)
    ]
    store_operand(dst, index, groups, low)


def put_warped(dst, index, padded, row, shift, low, sub):
    count = (padded.shape[1] - 2 * PAD) // SUB
    lanes = padded.shape[2]
    start = PAD - (shift >> 1)
    is_odd = (shift & 1) == 1
    raw = [
        padded[row, pl.ds(start + v, SUB, stride=count), :] for v in range(-2, count + 1)
    ]
    groups = []
    for v in range(1, len(raw)):
        odd = pltpu.roll(jnp.where(low, raw[v], raw[v - 1]), lanes // 2, 1)
        groups.append(jnp.where(is_odd, odd, raw[v]))
    groups[0] = jnp.where(sub > 0, groups[0], 0.0)
    groups[-1] = jnp.where(sub < SUB - 1, groups[-1], 0.0)
    store_operand(dst, index, groups, low)


def two_row_weight(w_ref, layers):
    zero = jnp.zeros(w_ref.shape[2:], BF16)
    upper, lower = [], []
    for layer in layers:
        w = [w_ref[layer, a] for a in range(3)]
        upper += w + [zero]
        lower += [zero] + w
    return jnp.concatenate(
        [jnp.concatenate(upper, axis=1), jnp.concatenate(lower, axis=1)], axis=0
    )


def two_row_conv(fetches, first, count, w_ref, layers):
    columns = []
    for fetch in fetches:
        for i in range(4):
            for part in range(2):
                columns.append(
                    jnp.concatenate(
                        [fetch(2 * (first + k) + i, part) for k in range(count)], axis=0
                    )
                )
    return lax.dot_general(
        jnp.concatenate(columns, axis=1),
        two_row_weight(w_ref, layers),
        (((1,), (1,)), ((), ())),
        preferred_element_type=F32,
    )


def scalars_of(row):
    half = row.shape[0] // 2
    wide = row.astype(F32)
    return (
        jnp.max(wide[0:SUB]).astype(jnp.int32),
        jnp.max(wide[half : half + SUB]).astype(jnp.int32),
    )


def local_span(band_rows):
    return (RIM + 1) // 2, (RIM + band_rows - 4) // 2 + 1


def clear_pads(padded):
    rows, long, lanes = padded.shape
    for row in range(rows):
        padded[row, 0:PAD, :] = jnp.zeros((PAD, lanes), F32)
        padded[row, long - PAD :, :] = jnp.zeros((PAD, lanes), F32)


class Place:
    def __init__(self, index, clip, slots):
        bands = slots // SECTIONS
        position = lax.rem(index[0] + (slots - bands // 2), slots)
        self.band = lax.rem(position, bands)
        self.owner = lax.div(position, bands)
        self.clip = clip
        self.even = lax.rem(self.band, 2) == 0
        self.above = self.band > 0
        self.below = self.band < bands - 1

    def keep(self, tick):
        return self.clip[lax.rem(self.owner + tick, SECTIONS)] != tick


def natural_to_rows(scratch, block):
    rows = block.shape[0]
    lanes = scratch.shape[1]
    pairs = block.shape[1] // lanes
    pitch = scratch.shape[0] // rows
    for p in range(pairs):
        tile = block[:, p * lanes : (p + 1) * lanes].astype(F32)
        scratch[pl.ds(p, rows, stride=pitch), :] = tile
    return [scratch[r * pitch : r * pitch + pairs, :].astype(BF16) for r in range(rows)]


def shift_row(flow, tick, pairs, lanes):
    halves = [
        jnp.full((pairs // 2, lanes), flow[0, which, tick].astype(F32)) for which in range(2)
    ]
    return jnp.concatenate(halves, axis=0).astype(BF16)


def pack_kernel(
    slots, index, flow_in, carried, features, own, first_one, first_two, natural, scratch, sems,
    flow,
):
    _, rows, pairs, lanes = own.shape
    place = Place(index, None, slots)
    copies = [
        pltpu.make_async_copy(block, natural.at[part], sems.at[part])
        for part, block in enumerate((carried.at[0], carried.at[1], features.at[0]))
    ]
    copies.append(pltpu.make_async_copy(flow_in, flow, sems.at[3]))
    for copy in copies:
        copy.start()
    for part in range(3):
        copies[part].wait()
        for r, row in enumerate(natural_to_rows(scratch.at[part], natural.at[part])):
            own[part, r] = row
    copies[3].wait()
    mark = shift_row(flow, 0, pairs, lanes)
    first_one[3 * RIM] = mark
    first_two[3 * RIM] = mark
    for last, first, chosen in (
        (first_one, first_two, place.even),
        (first_two, first_one, jnp.logical_not(place.even)),
    ):

        @pl.when(chosen)
        def _():
            for part in range(3):
                last[part * RIM : (part + 1) * RIM] = own[part, rows - RIM : rows]
                first[part * RIM : (part + 1) * RIM] = own[part, 0:RIM]


def frame_kernel(tick, flow_in, features, frame, natural, scratch, sems, flow):
    _, pairs, lanes = frame.shape
    rows = frame.shape[0] - 2
    copies = [
        pltpu.make_async_copy(features.at[tick], natural, sems.at[0]),
        pltpu.make_async_copy(flow_in, flow, sems.at[1]),
    ]
    for copy in copies:
        copy.start()
    copies[0].wait()
    for r, row in enumerate(natural_to_rows(scratch, natural)):
        frame[1 + r] = row
    copies[1].wait()
    mark = shift_row(flow, tick, pairs, lanes)
    frame[0] = mark
    frame[rows + 1] = mark


def own_terms(sources, w_ref, acc, ops, padded, low, sub):
    rows = ops.shape[1]
    at = 0
    for part, (row, shift, interleaved) in enumerate(sources):
        for r in range(rows):
            stage(padded, at, row(r), interleaved)
            if shift is None:
                put_plain(ops, (part, r), padded, at, low)
            else:
                put_warped(ops, (part, r), padded, at, shift, low, sub)
            at += 1
    first, end = local_span(rows)
    fetches = [lambda r, h, part=part: ops[part, r - RIM, h] for part in range(3)]
    acc[...] = two_row_conv(fetches, first, end - first, w_ref, (0, 1, 2))


def start_kernel(slots, index, clip, flow, own, w_ref, acc, ops, padded):
    lanes = own.shape[3]
    keep = Place(index, clip, slots).keep(0)
    clear_pads(padded)

    def kept(part):
        return lambda r: jnp.where(keep, own[part, r].astype(F32), 0.0)

    own_terms(
        (
            (kept(0), flow[0, 0, 0], False),
            (kept(1), flow[0, 1, 0], False),
            (lambda r: own[2, r].astype(F32), None, False),
        ),
        w_ref, acc, ops, padded, lane_low(lanes), sublane(lanes),
    )


def ahead_kernel(
    slots, tick, index, clip, latest, prev, feat, w_ref, acc, ops, natural, padded, plain_rows,
    *copying,
):
    rows, _, lanes = latest.shape
    place = Place(index, clip, slots)
    keep_latest = place.keep(tick)
    keep_earlier = keep_latest & place.keep(tick - 1)
    shift = scalars_of(feat[0])
    clear_pads(padded)
    for r in range(rows):
        plain_rows[r] = latest[r].astype(F32)
    own_terms(
        (
            (lambda r: jnp.where(keep_latest, plain_rows[r], 0.0), shift[0], True),
            (lambda r: jnp.where(keep_earlier, prev[r].astype(F32), 0.0), shift[1], tick > 1),
            (lambda r: feat[1 + r].astype(F32), None, False),
        ),
        w_ref, acc, ops, padded, lane_low(lanes), sublane(lanes),
    )
    if copying:
        natural_rows, sem = copying
        rows_to_natural(natural_rows, plain_rows)
        copy = pltpu.make_async_copy(natural_rows, natural.at[0], sem)
        copy.start()
        copy.wait()
    else:
        rows_to_natural(natural, plain_rows)


def rows_to_natural(natural, plain_rows):
    rows, pairs, lanes = plain_rows.shape
    groups = pairs // SUB
    flat = plain_rows.reshape(rows * pairs, lanes)
    for v in range(groups):
        for s in range(SUB):
            pair = groups * s + v
            tile = flat[pl.ds(SUB * v + s, rows, stride=pairs), :]
            natural[:, pair * lanes : (pair + 1) * lanes] = tile.astype(BF16)


def finish_kernel(
    slots, tick, index, clip, acc_in, ops, halo_one, halo_two, prev, w_ref,
    latest, natural, sends, window, layers, padded, plain_rows,
):
    parts, rows, _, pairs, lanes = ops.shape
    place = Place(index, clip, slots)
    even = place.even
    low, sub = lane_low(lanes), sublane(lanes)
    keep = place.keep(tick)
    keep_both = keep if tick == 0 else keep & place.keep(tick - 1)

    def above(r, one=halo_one, two=halo_two):
        return jnp.where(even, two[r], one[r])

    def below(r, one=halo_one, two=halo_two):
        return jnp.where(even, one[r], two[r])

    if tick == 0:
        marks = 3 * RIM
        sides = [
            (side, [lambda r, k=k, side=side: side(k * RIM + r) for k in range(3)],
             scalars_of(side(marks)))
            for side in (above, below)
        ]
    else:
        sides = [
            (
                side,
                [
                    lambda r, side=side: side(r),
                    lambda r, side=side: side(r, *prev),
                    lambda r, side=side, skip=skip: side(RIM + skip + r),
                ],
                scalars_of(side(mark)),
            )
            for side, skip, mark in ((above, 0, 2 * RIM), (below, 1, RIM))
        ]
    clear_pads(padded)
    at = 0
    for which, (side, sources, shift) in enumerate(sides):
        inside = place.above if which == 0 else place.below
        for r in range(RIM):
            for part in range(parts):
                row = sources[part](r).astype(F32)
                ok = inside & (keep, keep_both)[part] if part < 2 else inside
                interleaved = tick > part and part < 2
                stage(padded, at, jnp.where(ok, row, 0.0), interleaved)
                slot = which * RIM + r
                if part < 2:
                    put_warped(window, (part, slot), padded, at, shift[part], low, sub)
                else:
                    put_plain(window, (part, slot), padded, at, low)
                at += 1

    def operand(part):
        def fetch(r, h):
            if r < RIM:
                return window[part, r, h]
            if r < RIM + rows:
                return ops[part, r - RIM, h]
            return window[part, r - rows, h]

        return fetch

    count = (rows + 2 * RIM - 2) // 2
    first, end = local_span(rows)
    split = end

    def emit(layer, pair, both):
        margin = RIM - 1 - layer
        for q in range(2):
            r = 2 * pair + q
            value = both[:, q * lanes : (q + 1) * lanes]
            if layer == 0:
                value = jnp.maximum(value, 0.1 * value)
            elif layer % 2 == 1:
                value = jnp.maximum(value, 0.0)
            else:
                value = value + layers[layer - 2][r + 2, 0].astype(F32)
            if r < margin:
                value = jnp.where(place.above, value, 0.0)
            elif r >= margin + rows:
                value = jnp.where(place.below, value, 0.0)
            if layer < 2 * RES_BLOCKS:
                put(layers[layer], (r,), value, low, sub)
            else:
                if sends:
                    latest[r] = value.astype(BF16)
                else:
                    plain_rows[r] = value

    fetches = [operand(part) for part in range(parts)]
    join = tuple(range(parts))
    for begin, stop in ((0, first), (first, end), (end, count)):
        made = None
        if begin != first:
            made = two_row_conv(fetches, begin, stop - begin, w_ref, join)
        for k in range(begin, stop):
            source = acc_in if begin == first else made
            emit(0, k, source[(k - begin) * pairs : (k - begin + 1) * pairs])
    for layer in range(1, 2 * RES_BLOCKS + 1):
        count -= 1
        split -= 1
        for begin, stop in ((0, split), (split, count)):
            made = two_row_conv(
                [lambda r, h: layers[layer - 1][r, h]], begin, stop - begin, w_ref, (2 + layer,)
            )
            for k in range(begin, stop):
                emit(layer, k, made[(k - begin) * pairs : (k - begin + 1) * pairs])
    if not sends:
        rows_to_natural(natural, plain_rows)
        return
    send_one, send_two = sends

    @pl.when(even)
    def _():
        send_one[...] = latest[rows - RIM : rows]
        send_two[...] = latest[0:RIM]

    @pl.when(jnp.logical_not(even))
    def _():
        send_one[...] = latest[0:RIM]
        send_two[...] = latest[rows - RIM : rows]


def weight_kernel(join, res, w_ref):
    channels = join.shape[1]
    zero = jnp.zeros((channels, channels), F32)

    def fill(layer, a, taps):
        before, here, after = taps
        w_ref[layer, a, 0:channels] = jnp.concatenate([here, after, zero, before], axis=1).astype(
            BF16
        )
        w_ref[layer, a, channels : 2 * channels] = jnp.concatenate(
            [before, here, after, zero], axis=1
        ).astype(BF16)

    for a in range(3):
        whole = join[a].astype(F32)
        for part in range(3):
            starts = [(3 * b + part) * channels for b in range(3)]
            fill(part, a, [whole[:, at : at + channels] for at in starts])
    for layer in range(res.shape[0]):
        for a in range(3):
            whole = res[layer, a].astype(F32)
            fill(3 + layer, a, [whole[:, b * channels : (b + 1) * channels] for b in range(3)])


def shards(features, carried, flow_shift, clip_start, join_weight, res_weight):
    rows = features.shape[1]
    wide = features.shape[2]
    channels = join_weight.shape[2]
    lanes = 2 * channels
    pairs = wide // lanes
    slots = lax.axis_size("rows")
    bands = slots // SECTIONS
    lead = bands // 2
    index = lax.axis_index("rows")
    even = (index + (slots - lead)) % 2 == 0
    index = index.astype(jnp.int32).reshape(1)

    def route(move):
        return [(i, move(i) % slots) for i in range(slots)]

    def is_even(i):
        return (i - lead) % 2 == 0

    swap_one = route(lambda i: i + 1 if is_even(i) else i - 1)
    swap_two = route(lambda i: i - 1 if is_even(i) else i + 1)

    def shift_by(count):
        return route(lambda i: i + count)

    def send(block, path):
        return lax.ppermute(block, "rows", path)

    flow = jnp.transpose(flow_shift, (1, 2, 0))
    made = rows + 2 * (RIM - 1)
    long = pairs + 2 * PAD
    first, end = local_span(rows)
    params = pltpu.CompilerParams(vmem_limit_bytes=GRANT)

    def cost(pairs_done, depth):
        return pl.CostEstimate(
            flops=pairs_done * pairs * depth * 16 * lanes * lanes,
            bytes_accessed=4 << 20,
            transcendentals=0,
        )

    def operands(*lead_shape):
        return lead_shape + (2, pairs, lanes)

    def pack():
        def kernel(*refs):
            pack_kernel(slots, *refs)

        halo = jax.ShapeDtypeStruct((3 * RIM + 1, pairs, lanes), BF16)
        return pl.pallas_call(
            kernel,
            out_shape=(jax.ShapeDtypeStruct((3, rows, pairs, lanes), BF16), halo, halo),
            in_specs=[SMEM, HBM, HBM, HBM],
            out_specs=(VMEM, VMEM, VMEM),
            scratch_shapes=[
                pltpu.VMEM((3, rows, wide), BF16),
                pltpu.VMEM((3, rows * (pairs + SUB), lanes), F32),
                pltpu.SemaphoreType.DMA((4,)),
                pltpu.SMEM(flow.shape, jnp.int32),
            ],
            compiler_params=params,
            name="pack",
        )(index, in_hbm(flow), in_hbm(carried), in_hbm(features))

    def framed(tick, features):
        def kernel(*refs):
            frame_kernel(tick, *refs)

        return pl.pallas_call(
            kernel,
            out_shape=jax.ShapeDtypeStruct((rows + 2, pairs, lanes), BF16),
            in_specs=[HBM, HBM],
            out_specs=VMEM,
            scratch_shapes=[
                pltpu.VMEM((rows, wide), BF16),
                pltpu.VMEM((rows * (pairs + SUB), lanes), F32),
                pltpu.SemaphoreType.DMA((2,)),
                pltpu.SMEM(flow.shape, jnp.int32),
            ],
            compiler_params=params,
        )(in_hbm(flow), in_hbm(features))

    def start(own):
        def kernel(*refs):
            start_kernel(slots, *refs)

        return pl.pallas_call(
            kernel,
            out_shape=(
                jax.ShapeDtypeStruct(((end - first) * pairs, 2 * lanes), F32),
                jax.ShapeDtypeStruct(operands(3, rows), BF16),
            ),
            in_specs=[SMEM, SMEM, SMEM, VMEM, VMEM],
            out_specs=(VMEM, VMEM),
            scratch_shapes=[pltpu.VMEM((3 * rows, long, lanes), F32)],
            compiler_params=params,
            cost_estimate=cost(end - first, 3),
            name="start",
        )(index, clip_start, flow, own, weights)

    def ahead(tick, latest, prev, feat):
        def kernel(*refs):
            ahead_kernel(slots, tick, *refs)

        whole = (TICKS,) if tick == 1 else ()
        return pl.pallas_call(
            kernel,
            out_shape=(
                jax.ShapeDtypeStruct(((end - first) * pairs, 2 * lanes), F32),
                jax.ShapeDtypeStruct(operands(3, rows), BF16),
                jax.ShapeDtypeStruct(whole + (rows, wide), BF16),
            ),
            in_specs=[SMEM, SMEM] + [VMEM] * 4,
            out_specs=(VMEM, VMEM, HBM if whole else VMEM),
            scratch_shapes=[
                pltpu.VMEM((3 * rows, long, lanes), F32),
                pltpu.VMEM((rows, pairs, lanes), F32),
            ]
            + ([pltpu.VMEM((rows, wide), BF16), pltpu.SemaphoreType.DMA] if whole else []),
            compiler_params=params,
            cost_estimate=cost(end - first, 3),
        )(index, clip_start, latest, prev, feat, weights)

    def finish(tick, acc, ops, one, two, prev=()):
        last = tick + 1 == TICKS
        parts = ops.shape[0]

        def kernel(index, clip, acc_in, ops, one, two, *rest):
            before, (w_ref, *rest) = rest[: len(prev)], rest[len(prev) :]
            if last:
                natural, *scratch = rest
                latest, sends = None, ()
            else:
                latest, send_one, send_two, *scratch = rest
                natural, sends = None, (send_one, send_two)
            window, *layers, padded, plain_rows = scratch
            finish_kernel(
                slots, tick, index, clip, acc_in, ops, one, two, before, w_ref,
                latest, natural, sends, window, layers, padded, plain_rows,
            )

        halo = jax.ShapeDtypeStruct((RIM, pairs, lanes), BF16)
        if last:
            outs = (jax.ShapeDtypeStruct((rows, wide), BF16),)
        else:
            outs = (jax.ShapeDtypeStruct((rows, pairs, lanes), BF16), halo, halo)
        return pl.pallas_call(
            kernel,
            out_shape=outs,
            in_specs=[SMEM, SMEM] + [VMEM] * (5 + len(prev)),
            out_specs=(VMEM,) * len(outs),
            scratch_shapes=[pltpu.VMEM(operands(parts, 2 * RIM), BF16)]
            + [pltpu.VMEM(operands(made - 2 * layer), BF16) for layer in range(2 * RES_BLOCKS)]
            + [
                pltpu.VMEM((parts * 2 * RIM, long, lanes), F32),
                pltpu.VMEM((rows, pairs, lanes), F32),
            ],
            compiler_params=params,
            cost_estimate=cost(made + made // 2 * parts, 1),
        )(index, clip_start, acc, ops, one, two, *prev, weights)

    own, first_one, first_two = pack()
    later_features, first_one, first_two = lax.optimization_barrier(
        (features, first_one, first_two)
    )
    halo_two = send(first_two, swap_two)
    halo_one = send(first_one, swap_one)
    frame = framed(1, later_features)
    frame, own, join_weight, res_weight = lax.optimization_barrier(
        (frame, own, join_weight, res_weight)
    )

    def bring(tick, frame):
        return send(frame, shift_by(-bands * tick))

    feat = bring(1, frame)
    weights = pl.pallas_call(
        weight_kernel,
        out_shape=jax.ShapeDtypeStruct((3 + 2 * RES_BLOCKS, 3, lanes, 2 * lanes), BF16),
        in_specs=[VMEM, VMEM],
        out_specs=VMEM,
        compiler_params=params,
        name="weights",
    )(jnp.transpose(join_weight, (0, 2, 1)), jnp.transpose(res_weight, (0, 1, 3, 2)))
    acc, ops = start(own)
    begin_one = jnp.where(even, rows + 1 - RIM, 0)
    begin_two = jnp.where(even, 0, rows + 1 - RIM)

    def with_rim(block, frame, begin):
        return jnp.concatenate(
            [block, lax.dynamic_slice_in_dim(frame, begin, RIM + 1, axis=0)], axis=0
        )

    last_features, acc = lax.optimization_barrier((later_features, acc))
    second_feat = bring(2, framed(2, last_features))
    one, two = halo_one, halo_two
    prev = own[0]
    outs = finish(0, acc, ops, one, two)
    for tick in range(1, TICKS):
        latest, send_one, send_two = outs
        feat, latest, send_one, send_two = lax.optimization_barrier(
            (feat, latest, send_one, send_two)
        )
        before = one, two
        two = send(with_rim(send_two, feat, begin_two), swap_two)
        one = send(with_rim(send_one, feat, begin_one), swap_one)
        acc, ops, natural = ahead(tick, latest, prev, feat)
        if tick == 1:
            result = natural
        else:
            moved = send(natural, shift_by(bands * (tick - 1)))
            result = lax.dynamic_update_slice_in_dim(result, moved[None], tick - 1, 0)
        prev = latest
        feat = second_feat
        outs = finish(tick, acc, ops, one, two, before)
    moved = send(outs[0], shift_by(bands * (TICKS - 1)))
    return lax.dynamic_update_slice_in_dim(result, moved[None], TICKS - 1, 0)


def solution(mesh):
    in_specs = (
        P(None, ("groups", "rows"), None),
        P(None, ("groups", "rows"), None),
        P(None, ("groups", "rows"), None),
        P("groups"),
        P(),
        P(),
    )
    out_specs = P(None, ("groups", "rows"), None)

    return jax.shard_map(
        shards, mesh=mesh, in_specs=in_specs, out_specs=out_specs, check_vma=False
    )
```

```python
import jax
import jax.numpy as jnp
from jax import lax
from jax.experimental import pallas as pl
from jax.experimental.pallas import tpu as pltpu
from jax.sharding import PartitionSpec as P


TICKS = 3
SECTIONS = 4
RES_BLOCKS = 2
RIM = 1 + 2 * RES_BLOCKS
PAD = 8
SUB = 8
GRANT = 24 << 20

BF16 = jnp.bfloat16
F32 = jnp.float32
VMEM = pl.BlockSpec(memory_space=pltpu.VMEM)
SMEM = pl.BlockSpec(memory_space=pltpu.SMEM)
HBM = pl.BlockSpec(memory_space=pltpu.HBM)


def in_hbm(block):
    return pltpu.with_memory_space_constraint(block, pltpu.HBM)


def lane_low(lanes):
    return lax.broadcasted_iota(jnp.int32, (SUB, lanes), 1) < lanes // 2


def sublane(lanes):
    return lax.broadcasted_iota(jnp.int32, (SUB, lanes), 0)


def store_operand(dst, index, groups, low):
    here = jnp.concatenate(groups[1:-1], axis=0)
    beside = jnp.concatenate(
        [jnp.where(low, groups[v + 2], groups[v]) for v in range(len(groups) - 2)], axis=0
    )
    dst[index + (0,)] = here.astype(BF16)
    dst[index + (1,)] = beside.astype(BF16)


def put(dst, index, row, low, sub):
    count = row.shape[0] // SUB
    groups = [row[SUB * v : SUB * v + SUB] for v in range(count)]
    before = jnp.where(sub > 0, pltpu.roll(groups[-1], 1, 0), 0.0)
    after = jnp.where(sub < SUB - 1, pltpu.roll(groups[0], SUB - 1, 0), 0.0)
    store_operand(dst, index, [before] + groups + [after], low)


def stage(padded, row, value, interleaved):
    pairs = value.shape[0]
    count = pairs // SUB
    if interleaved:
        for v in range(count):
            padded[row, pl.ds(PAD + v, SUB, stride=count), :] = value[SUB * v : SUB * v + SUB]
    else:
        padded[row, PAD : PAD + pairs, :] = value


def put_plain(dst, index, padded, row, low):
    count = (padded.shape[1] - 2 * PAD) // SUB
    groups = [
        padded[row, pl.ds(PAD + v, SUB, stride=count), :] for v in range(-1, count + 1)
    ]
    store_operand(dst, index, groups, low)


def put_warped(dst, index, padded, row, shift, low, sub):
    count = (padded.shape[1] - 2 * PAD) // SUB
    lanes = padded.shape[2]
    start = PAD - (shift >> 1)
    is_odd = (shift & 1) == 1
    raw = [
        padded[row, pl.ds(start + v, SUB, stride=count), :] for v in range(-2, count + 1)
    ]
    groups = []
    for v in range(1, len(raw)):
        odd = pltpu.roll(jnp.where(low, raw[v], raw[v - 1]), lanes // 2, 1)
        groups.append(jnp.where(is_odd, odd, raw[v]))
    groups[0] = jnp.where(sub > 0, groups[0], 0.0)
    groups[-1] = jnp.where(sub < SUB - 1, groups[-1], 0.0)
    store_operand(dst, index, groups, low)


def two_row_weight(w_ref, layers):
    zero = jnp.zeros(w_ref.shape[2:], BF16)
    upper, lower = [], []
    for layer in layers:
        w = [w_ref[layer, a] for a in range(3)]
        upper += w + [zero]
        lower += [zero] + w
    return jnp.concatenate(
        [jnp.concatenate(upper, axis=1), jnp.concatenate(lower, axis=1)], axis=0
    )


def two_row_conv(fetches, first, count, w_ref, layers):
    columns = []
    for fetch in fetches:
        for i in range(4):
            for part in range(2):
                columns.append(
                    jnp.concatenate(
                        [fetch(2 * (first + k) + i, part) for k in range(count)], axis=0
                    )
                )
    return lax.dot_general(
        jnp.concatenate(columns, axis=1),
        two_row_weight(w_ref, layers),
        (((1,), (1,)), ((), ())),
        preferred_element_type=F32,
    )


def scalars_of(row):
    half = row.shape[0] // 2
    wide = row.astype(F32)
    return (
        jnp.max(wide[0:SUB]).astype(jnp.int32),
        jnp.max(wide[half : half + SUB]).astype(jnp.int32),
    )


def local_span(band_rows):
    return (RIM + 1) // 2, (RIM + band_rows - 4) // 2 + 1


def clear_pads(padded):
    rows, long, lanes = padded.shape
    for row in range(rows):
        padded[row, 0:PAD, :] = jnp.zeros((PAD, lanes), F32)
        padded[row, long - PAD :, :] = jnp.zeros((PAD, lanes), F32)


class Place:
    def __init__(self, index, clip, slots):
        bands = slots // SECTIONS
        position = lax.rem(index[0] + (slots - bands // 2), slots)
        self.band = lax.rem(position, bands)
        self.owner = lax.div(position, bands)
        self.clip = clip
        self.even = lax.rem(self.band, 2) == 0
        self.above = self.band > 0
        self.below = self.band < bands - 1

    def keep(self, tick):
        return self.clip[lax.rem(self.owner + tick, SECTIONS)] != tick


def natural_to_rows(scratch, block):
    rows = block.shape[0]
    lanes = scratch.shape[1]
    pairs = block.shape[1] // lanes
    pitch = scratch.shape[0] // rows
    for p in range(pairs):
        tile = block[:, p * lanes : (p + 1) * lanes].astype(F32)
        scratch[pl.ds(p, rows, stride=pitch), :] = tile
    return [scratch[r * pitch : r * pitch + pairs, :].astype(BF16) for r in range(rows)]


def shift_row(flow, tick, pairs, lanes):
    halves = [
        jnp.full((pairs // 2, lanes), flow[0, which, tick].astype(F32)) for which in range(2)
    ]
    return jnp.concatenate(halves, axis=0).astype(BF16)


def pack_kernel(
    slots, index, flow_in, carried, features, own, first_one, first_two, natural, scratch, sems,
    flow,
):
    _, rows, pairs, lanes = own.shape
    place = Place(index, None, slots)
    copies = [
        pltpu.make_async_copy(block, natural.at[part], sems.at[part])
        for part, block in enumerate((carried.at[0], carried.at[1], features.at[0]))
    ]
    copies.append(pltpu.make_async_copy(flow_in, flow, sems.at[3]))
    for copy in copies:
        copy.start()
    for part in range(3):
        copies[part].wait()
        for r, row in enumerate(natural_to_rows(scratch.at[part], natural.at[part])):
            own[part, r] = row
    copies[3].wait()
    mark = shift_row(flow, 0, pairs, lanes)
    first_one[3 * RIM] = mark
    first_two[3 * RIM] = mark
    for last, first, chosen in (
        (first_one, first_two, place.even),
        (first_two, first_one, jnp.logical_not(place.even)),
    ):

        @pl.when(chosen)
        def _():
            for part in range(3):
                last[part * RIM : (part + 1) * RIM] = own[part, rows - RIM : rows]
                first[part * RIM : (part + 1) * RIM] = own[part, 0:RIM]


def frame_kernel(tick, flow_in, features, frame, natural, scratch, sems, flow):
    _, pairs, lanes = frame.shape
    copies = [
        pltpu.make_async_copy(features.at[tick], natural, sems.at[0]),
        pltpu.make_async_copy(flow_in, flow, sems.at[1]),
    ]
    for copy in copies:
        copy.start()
    copies[0].wait()
    for r, row in enumerate(natural_to_rows(scratch, natural)):
        frame[1 + r] = row
    copies[1].wait()
    frame[0] = shift_row(flow, tick, pairs, lanes)


def own_terms(sources, w_ref, acc, ops, padded, low, sub):
    rows = ops.shape[1]
    at = 0
    for part, (row, shift, interleaved) in enumerate(sources):
        for r in range(rows):
            stage(padded, at, row(r), interleaved)
            if shift is None:
                put_plain(ops, (part, r), padded, at, low)
            else:
                put_warped(ops, (part, r), padded, at, shift, low, sub)
            at += 1
    first, end = local_span(rows)
    fetches = [lambda r, h, part=part: ops[part, r - RIM, h] for part in range(3)]
    acc[...] = two_row_conv(fetches, first, end - first, w_ref, (0, 1, 2))


def start_kernel(slots, index, clip, flow, own, w_ref, acc, ops, padded):
    lanes = own.shape[3]
    keep = Place(index, clip, slots).keep(0)
    clear_pads(padded)

    def kept(part):
        return lambda r: jnp.where(keep, own[part, r].astype(F32), 0.0)

    own_terms(
        (
            (kept(0), flow[0, 0, 0], False),
            (kept(1), flow[0, 1, 0], False),
            (lambda r: own[2, r].astype(F32), None, False),
        ),
        w_ref, acc, ops, padded, lane_low(lanes), sublane(lanes),
    )


def ahead_kernel(
    slots, tick, index, clip, latest, prev, feat, w_ref, acc, ops, natural, padded, plain_rows,
    *copying,
):
    rows, _, lanes = latest.shape
    place = Place(index, clip, slots)
    keep_latest = place.keep(tick)
    keep_earlier = keep_latest & place.keep(tick - 1)
    shift = scalars_of(feat[0])
    clear_pads(padded)
    for r in range(rows):
        plain_rows[r] = latest[r].astype(F32)
    own_terms(
        (
            (lambda r: jnp.where(keep_latest, plain_rows[r], 0.0), shift[0], True),
            (lambda r: jnp.where(keep_earlier, prev[r].astype(F32), 0.0), shift[1], tick > 1),
            (lambda r: feat[1 + r].astype(F32), None, False),
        ),
        w_ref, acc, ops, padded, lane_low(lanes), sublane(lanes),
    )
    if copying:
        natural_rows, sem = copying
        rows_to_natural(natural_rows, plain_rows)
        copy = pltpu.make_async_copy(natural_rows, natural.at[0], sem)
        copy.start()
        copy.wait()
    else:
        rows_to_natural(natural, plain_rows)


def rows_to_natural(natural, plain_rows):
    rows, pairs, lanes = plain_rows.shape
    groups = pairs // SUB
    flat = plain_rows.reshape(rows * pairs, lanes)
    for v in range(groups):
        for s in range(SUB):
            pair = groups * s + v
            tile = flat[pl.ds(SUB * v + s, rows, stride=pairs), :]
            natural[:, pair * lanes : (pair + 1) * lanes] = tile.astype(BF16)


def finish_kernel(
    slots, tick, index, clip, acc_in, ops, halo_one, halo_two, prev, w_ref,
    latest, natural, sends, window, layers, padded, plain_rows,
):
    _, rows, _, pairs, lanes = ops.shape
    place = Place(index, clip, slots)
    even = place.even
    low, sub = lane_low(lanes), sublane(lanes)
    keep = place.keep(tick)
    keep_both = keep if tick == 0 else keep & place.keep(tick - 1)

    def above(r, one=halo_one, two=halo_two):
        return jnp.where(even, two[r], one[r])

    def below(r, one=halo_one, two=halo_two):
        return jnp.where(even, one[r], two[r])

    if tick == 0:
        marks = 3 * RIM
        sides = [
            (side, [lambda r, k=k, side=side: side(k * RIM + r) for k in range(3)],
             scalars_of(side(marks)))
            for side in (above, below)
        ]
    else:
        sides = [
            (
                side,
                [
                    lambda r, side=side: side(r),
                    lambda r, side=side: side(r, *prev),
                    lambda r, side=side: side(RIM + 1 + r),
                ],
                scalars_of(side(RIM)),
            )
            for side in (above, below)
        ]

    def operand(part):
        def fetch(r, h):
            if r < RIM:
                return window[part, r, h]
            if r < RIM + rows:
                return ops[part, r - RIM, h]
            return window[part, r - rows, h]

        return fetch

    count = (rows + 2 * RIM - 2) // 2
    first, end = local_span(rows)
    split = end
    clear_pads(padded)
    at = 0
    terms = {}
    for part in (2, 0, 1):
        for which, (side, sources, shift) in enumerate(sides):
            ok = place.above if which == 0 else place.below
            if part < 2:
                ok = ok & (keep, keep_both)[part]
            for r in range(RIM):
                row = sources[part](r).astype(F32)
                stage(padded, at, jnp.where(ok, row, 0.0), tick > part and part < 2)
                slot = which * RIM + r
                if part < 2:
                    put_warped(window, (part, slot), padded, at, shift[part], low, sub)
                else:
                    put_plain(window, (part, slot), padded, at, low)
                at += 1
            begin, stop = ((0, first), (end, count))[which]
            term = two_row_conv([operand(part)], begin, stop - begin, w_ref, (part,))
            terms[begin] = terms[begin] + term if begin in terms else term


    def emit(layer, pair, both):
        margin = RIM - 1 - layer
        for q in range(2):
            r = 2 * pair + q
            value = both[:, q * lanes : (q + 1) * lanes]
            if layer == 0:
                value = jnp.maximum(value, 0.1 * value)
            elif layer % 2 == 1:
                value = jnp.maximum(value, 0.0)
            else:
                value = value + layers[layer - 2][r + 2, 0].astype(F32)
            if r < margin:
                value = jnp.where(place.above, value, 0.0)
            elif r >= margin + rows:
                value = jnp.where(place.below, value, 0.0)
            if layer < 2 * RES_BLOCKS:
                put(layers[layer], (r,), value, low, sub)
            else:
                if sends:
                    latest[r] = value.astype(BF16)
                else:
                    plain_rows[r] = value

    for begin, stop in ((0, first), (first, end), (end, count)):
        for k in range(begin, stop):
            source = acc_in if begin == first else terms[begin]
            emit(0, k, source[(k - begin) * pairs : (k - begin + 1) * pairs])
    for layer in range(1, 2 * RES_BLOCKS + 1):
        count -= 1
        split -= 1
        for begin, stop in ((0, split), (split, count)):
            made = two_row_conv(
                [lambda r, h: layers[layer - 1][r, h]], begin, stop - begin, w_ref, (2 + layer,)
            )
            for k in range(begin, stop):
                emit(layer, k, made[(k - begin) * pairs : (k - begin + 1) * pairs])
    if not sends:
        rows_to_natural(natural, plain_rows)
        return
    send_one, send_two = sends

    @pl.when(even)
    def _():
        send_one[...] = latest[rows - RIM : rows]
        send_two[...] = latest[0:RIM]

    @pl.when(jnp.logical_not(even))
    def _():
        send_one[...] = latest[0:RIM]
        send_two[...] = latest[rows - RIM : rows]


def weight_kernel(join, res, w_ref):
    channels = join.shape[1]
    zero = jnp.zeros((channels, channels), F32)

    def fill(layer, a, taps):
        before, here, after = taps
        w_ref[layer, a, 0:channels] = jnp.concatenate([here, after, zero, before], axis=1).astype(
            BF16
        )
        w_ref[layer, a, channels : 2 * channels] = jnp.concatenate(
            [before, here, after, zero], axis=1
        ).astype(BF16)

    for a in range(3):
        whole = join[a].astype(F32)
        for part in range(3):
            starts = [(3 * b + part) * channels for b in range(3)]
            fill(part, a, [whole[:, at : at + channels] for at in starts])
    for layer in range(res.shape[0]):
        for a in range(3):
            whole = res[layer, a].astype(F32)
            fill(3 + layer, a, [whole[:, b * channels : (b + 1) * channels] for b in range(3)])


def shards(features, carried, flow_shift, clip_start, join_weight, res_weight):
    rows = features.shape[1]
    wide = features.shape[2]
    channels = join_weight.shape[2]
    lanes = 2 * channels
    pairs = wide // lanes
    slots = lax.axis_size("rows")
    bands = slots // SECTIONS
    lead = bands // 2
    index = lax.axis_index("rows")
    even = (index + (slots - lead)) % 2 == 0
    index = index.astype(jnp.int32).reshape(1)

    def route(move):
        return [(i, move(i) % slots) for i in range(slots)]

    def is_even(i):
        return (i - lead) % 2 == 0

    swap_one = route(lambda i: i + 1 if is_even(i) else i - 1)
    swap_two = route(lambda i: i - 1 if is_even(i) else i + 1)

    def shift_by(count):
        return route(lambda i: i + count)

    def send(block, path):
        return lax.ppermute(block, "rows", path)

    flow = jnp.transpose(flow_shift, (1, 2, 0))
    made = rows + 2 * (RIM - 1)
    long = pairs + 2 * PAD
    first, end = local_span(rows)
    params = pltpu.CompilerParams(vmem_limit_bytes=GRANT)

    def cost(pairs_done, depth):
        return pl.CostEstimate(
            flops=pairs_done * pairs * depth * 16 * lanes * lanes,
            bytes_accessed=4 << 20,
            transcendentals=0,
        )

    def operands(*lead_shape):
        return lead_shape + (2, pairs, lanes)

    def pack():
        def kernel(*refs):
            pack_kernel(slots, *refs)

        halo = jax.ShapeDtypeStruct((3 * RIM + 1, pairs, lanes), BF16)
        return pl.pallas_call(
            kernel,
            out_shape=(jax.ShapeDtypeStruct((3, rows, pairs, lanes), BF16), halo, halo),
            in_specs=[SMEM, HBM, HBM, HBM],
            out_specs=(VMEM, VMEM, VMEM),
            scratch_shapes=[
                pltpu.VMEM((3, rows, wide), BF16),
                pltpu.VMEM((3, rows * (pairs + SUB), lanes), F32),
                pltpu.SemaphoreType.DMA((4,)),
                pltpu.SMEM(flow.shape, jnp.int32),
            ],
            compiler_params=params,
            name="pack",
        )(index, in_hbm(flow), in_hbm(carried), in_hbm(features))

    def framed(tick, features):
        def kernel(*refs):
            frame_kernel(tick, *refs)

        return pl.pallas_call(
            kernel,
            out_shape=jax.ShapeDtypeStruct((rows + 1, pairs, lanes), BF16),
            in_specs=[HBM, HBM],
            out_specs=VMEM,
            scratch_shapes=[
                pltpu.VMEM((rows, wide), BF16),
                pltpu.VMEM((rows * (pairs + SUB), lanes), F32),
                pltpu.SemaphoreType.DMA((2,)),
                pltpu.SMEM(flow.shape, jnp.int32),
            ],
            compiler_params=params,
        )(in_hbm(flow), in_hbm(features))

    def start(own):
        def kernel(*refs):
            start_kernel(slots, *refs)

        return pl.pallas_call(
            kernel,
            out_shape=(
                jax.ShapeDtypeStruct(((end - first) * pairs, 2 * lanes), F32),
                jax.ShapeDtypeStruct(operands(3, rows), BF16),
            ),
            in_specs=[SMEM, SMEM, SMEM, VMEM, VMEM],
            out_specs=(VMEM, VMEM),
            scratch_shapes=[pltpu.VMEM((3 * rows, long, lanes), F32)],
            compiler_params=params,
            cost_estimate=cost(end - first, 3),
            name="start",
        )(index, clip_start, flow, own, weights)

    def ahead(tick, latest, prev, feat):
        def kernel(*refs):
            ahead_kernel(slots, tick, *refs)

        whole = (TICKS,) if tick == 1 else ()
        return pl.pallas_call(
            kernel,
            out_shape=(
                jax.ShapeDtypeStruct(((end - first) * pairs, 2 * lanes), F32),
                jax.ShapeDtypeStruct(operands(3, rows), BF16),
                jax.ShapeDtypeStruct(whole + (rows, wide), BF16),
            ),
            in_specs=[SMEM, SMEM] + [VMEM] * 4,
            out_specs=(VMEM, VMEM, HBM if whole else VMEM),
            scratch_shapes=[
                pltpu.VMEM((3 * rows, long, lanes), F32),
                pltpu.VMEM((rows, pairs, lanes), F32),
            ]
            + ([pltpu.VMEM((rows, wide), BF16), pltpu.SemaphoreType.DMA] if whole else []),
            compiler_params=params,
            cost_estimate=cost(end - first, 3),
        )(index, clip_start, latest, prev, feat, weights)

    def finish(tick, acc, ops, one, two, prev=()):
        last = tick + 1 == TICKS
        parts = ops.shape[0]

        def kernel(index, clip, acc_in, ops, one, two, *rest):
            before, (w_ref, *rest) = rest[: len(prev)], rest[len(prev) :]
            if last:
                natural, *scratch = rest
                latest, sends = None, ()
            else:
                latest, send_one, send_two, *scratch = rest
                natural, sends = None, (send_one, send_two)
            window, *layers, padded, plain_rows = scratch
            finish_kernel(
                slots, tick, index, clip, acc_in, ops, one, two, before, w_ref,
                latest, natural, sends, window, layers, padded, plain_rows,
            )

        halo = jax.ShapeDtypeStruct((RIM, pairs, lanes), BF16)
        if last:
            outs = (jax.ShapeDtypeStruct((rows, wide), BF16),)
        else:
            outs = (jax.ShapeDtypeStruct((rows, pairs, lanes), BF16), halo, halo)
        return pl.pallas_call(
            kernel,
            out_shape=outs,
            in_specs=[SMEM, SMEM] + [VMEM] * (5 + len(prev)),
            out_specs=(VMEM,) * len(outs),
            scratch_shapes=[pltpu.VMEM(operands(parts, 2 * RIM), BF16)]
            + [pltpu.VMEM(operands(made - 2 * layer), BF16) for layer in range(2 * RES_BLOCKS)]
            + [
                pltpu.VMEM((parts * 2 * RIM, long, lanes), F32),
                pltpu.VMEM((rows, pairs, lanes), F32),
            ],
            compiler_params=params,
            cost_estimate=cost(made + made // 2 * parts, 1),
        )(index, clip_start, acc, ops, one, two, *prev, weights)

    own, first_one, first_two = pack()
    later_features, first_one, first_two = lax.optimization_barrier(
        (features, first_one, first_two)
    )
    halo_two = send(first_two, swap_two)
    halo_one = send(first_one, swap_one)
    frame = framed(1, later_features)
    frame, own, join_weight, res_weight = lax.optimization_barrier(
        (frame, own, join_weight, res_weight)
    )

    def bring(tick, frame):
        return send(frame, shift_by(-bands * tick))

    feat = bring(1, frame)
    weights = pl.pallas_call(
        weight_kernel,
        out_shape=jax.ShapeDtypeStruct((3 + 2 * RES_BLOCKS, 3, lanes, 2 * lanes), BF16),
        in_specs=[VMEM, VMEM],
        out_specs=VMEM,
        compiler_params=params,
        name="weights",
    )(jnp.transpose(join_weight, (0, 2, 1)), jnp.transpose(res_weight, (0, 1, 3, 2)))
    acc, ops = start(own)
    begin_one = jnp.where(even, rows + 1 - RIM, 1)
    begin_two = jnp.where(even, 1, rows + 1 - RIM)

    def with_rim(block, frame, begin):
        rim = lax.dynamic_slice_in_dim(frame, begin, RIM, axis=0)
        return jnp.concatenate([block, frame[0:1], rim], axis=0)

    last_features = later_features
    second_feat = bring(2, framed(2, last_features))
    one, two = halo_one, halo_two
    prev = own[0]
    outs = finish(0, acc, ops, one, two)
    for tick in range(1, TICKS):
        latest, send_one, send_two = outs
        feat, latest, send_one, send_two = lax.optimization_barrier(
            (feat, latest, send_one, send_two)
        )
        before = one, two
        two = send(with_rim(send_two, feat, begin_two), swap_two)
        one = send(with_rim(send_one, feat, begin_one), swap_one)
        acc, ops, natural = ahead(tick, latest, prev, feat)
        if tick == 1:
            result = natural
        else:
            moved = send(natural, shift_by(bands * (tick - 1)))
            result = lax.dynamic_update_slice_in_dim(result, moved[None], tick - 1, 0)
        prev = latest
        feat = second_feat
        outs = finish(tick, acc, ops, one, two, before)
    moved = send(outs[0], shift_by(bands * (TICKS - 1)))
    return lax.dynamic_update_slice_in_dim(result, moved[None], TICKS - 1, 0)


def solution(mesh):
    in_specs = (
        P(None, ("groups", "rows"), None),
        P(None, ("groups", "rows"), None),
        P(None, ("groups", "rows"), None),
        P("groups"),
        P(),
        P(),
    )
    out_specs = P(None, ("groups", "rows"), None)

    return jax.shard_map(
        shards, mesh=mesh, in_specs=in_specs, out_specs=out_specs, check_vma=False
    )
```

```python
import jax
import jax.numpy as jnp
from jax import lax
from jax.experimental import pallas as pl
from jax.experimental.pallas import tpu as pltpu
from jax.sharding import PartitionSpec as P


TICKS = 3
SECTIONS = 4
RES_BLOCKS = 2
RIM = 1 + 2 * RES_BLOCKS
PAD = 8
SUB = 8
GRANT = 24 << 20

BF16 = jnp.bfloat16
F32 = jnp.float32
VMEM = pl.BlockSpec(memory_space=pltpu.VMEM)
SMEM = pl.BlockSpec(memory_space=pltpu.SMEM)
HBM = pl.BlockSpec(memory_space=pltpu.HBM)


def in_hbm(block):
    return pltpu.with_memory_space_constraint(block, pltpu.HBM)


def lane_low(lanes):
    return lax.broadcasted_iota(jnp.int32, (SUB, lanes), 1) < lanes // 2


def sublane(lanes):
    return lax.broadcasted_iota(jnp.int32, (SUB, lanes), 0)


def store_operand(dst, index, groups, low):
    here = jnp.concatenate(groups[1:-1], axis=0)
    beside = jnp.concatenate(
        [jnp.where(low, groups[v + 2], groups[v]) for v in range(len(groups) - 2)], axis=0
    )
    dst[index + (0,)] = here.astype(BF16)
    dst[index + (1,)] = beside.astype(BF16)


def put(dst, index, row, low, sub):
    count = row.shape[0] // SUB
    groups = [row[SUB * v : SUB * v + SUB] for v in range(count)]
    before = jnp.where(sub > 0, pltpu.roll(groups[-1], 1, 0), 0.0)
    after = jnp.where(sub < SUB - 1, pltpu.roll(groups[0], SUB - 1, 0), 0.0)
    store_operand(dst, index, [before] + groups + [after], low)


def stage(padded, row, value, interleaved):
    pairs = value.shape[0]
    count = pairs // SUB
    if interleaved:
        for v in range(count):
            padded[row, pl.ds(PAD + v, SUB, stride=count), :] = value[SUB * v : SUB * v + SUB]
    else:
        padded[row, PAD : PAD + pairs, :] = value


def put_plain(dst, index, padded, row, low):
    count = (padded.shape[1] - 2 * PAD) // SUB
    groups = [
        padded[row, pl.ds(PAD + v, SUB, stride=count), :] for v in range(-1, count + 1)
    ]
    store_operand(dst, index, groups, low)


def put_warped(dst, index, padded, row, shift, low, sub):
    count = (padded.shape[1] - 2 * PAD) // SUB
    lanes = padded.shape[2]
    start = PAD - (shift >> 1)
    is_odd = (shift & 1) == 1
    raw = [
        padded[row, pl.ds(start + v, SUB, stride=count), :] for v in range(-2, count + 1)
    ]
    groups = []
    for v in range(1, len(raw)):
        odd = pltpu.roll(jnp.where(low, raw[v], raw[v - 1]), lanes // 2, 1)
        groups.append(jnp.where(is_odd, odd, raw[v]))
    groups[0] = jnp.where(sub > 0, groups[0], 0.0)
    groups[-1] = jnp.where(sub < SUB - 1, groups[-1], 0.0)
    store_operand(dst, index, groups, low)


def two_row_weight(w_ref, layers):
    rows = []
    for layer in layers:
        zero = jnp.zeros(w_ref.shape[2:], BF16)
        w = [w_ref[layer, a] for a in range(3)]
        for pair in ((w[0], zero), (w[1], w[0]), (w[2], w[1]), (zero, w[2])):
            rows.append(jnp.concatenate(pair, axis=1))
    return jnp.concatenate(rows, axis=0)


def two_row_conv(fetches, first, count, w_ref, layers):
    columns = []
    for fetch in fetches:
        for i in range(4):
            for part in range(2):
                columns.append(
                    jnp.concatenate(
                        [fetch(2 * (first + k) + i, part) for k in range(count)], axis=0
                    )
                )
    return lax.dot_general(
        jnp.concatenate(columns, axis=1),
        two_row_weight(w_ref, layers),
        (((1,), (0,)), ((), ())),
        preferred_element_type=F32,
    )


def scalars_of(row):
    half = row.shape[0] // 2
    wide = row.astype(F32)
    return (
        jnp.max(wide[0:SUB]).astype(jnp.int32),
        jnp.max(wide[half : half + SUB]).astype(jnp.int32),
    )


def local_span(band_rows):
    return (RIM + 1) // 2, (RIM + band_rows - 4) // 2 + 1


def clear_pads(padded):
    rows, long, lanes = padded.shape
    for row in range(rows):
        padded[row, 0:PAD, :] = jnp.zeros((PAD, lanes), F32)
        padded[row, long - PAD :, :] = jnp.zeros((PAD, lanes), F32)


class Place:
    def __init__(self, index, clip, slots):
        bands = slots // SECTIONS
        position = lax.rem(index[0] + (slots - bands // 2), slots)
        self.band = lax.rem(position, bands)
        self.owner = lax.div(position, bands)
        self.clip = clip
        self.even = lax.rem(self.band, 2) == 0
        self.above = self.band > 0
        self.below = self.band < bands - 1

    def keep(self, tick):
        return self.clip[lax.rem(self.owner + tick, SECTIONS)] != tick


def natural_to_rows(scratch, block):
    rows = block.shape[0]
    lanes = scratch.shape[1]
    pairs = block.shape[1] // lanes
    pitch = scratch.shape[0] // rows
    for p in range(pairs):
        tile = block[:, p * lanes : (p + 1) * lanes].astype(F32)
        scratch[pl.ds(p, rows, stride=pitch), :] = tile
    return [scratch[r * pitch : r * pitch + pairs, :].astype(BF16) for r in range(rows)]


def shift_row(flow, tick, pairs, lanes):
    halves = [
        jnp.full((pairs // 2, lanes), flow[0, which, tick].astype(F32)) for which in range(2)
    ]
    return jnp.concatenate(halves, axis=0).astype(BF16)


def pack_kernel(
    slots, index, flow_in, carried, features, own, first_one, first_two, natural, scratch, sems,
    flow,
):
    _, rows, pairs, lanes = own.shape
    place = Place(index, None, slots)
    copies = [
        pltpu.make_async_copy(block, natural.at[part], sems.at[part])
        for part, block in enumerate((carried.at[0], carried.at[1], features.at[0]))
    ]
    copies.append(pltpu.make_async_copy(flow_in, flow, sems.at[3]))
    for copy in copies:
        copy.start()
    for part in range(3):
        copies[part].wait()
        for r, row in enumerate(natural_to_rows(scratch.at[part], natural.at[part])):
            own[part, r] = row
    copies[3].wait()
    mark = shift_row(flow, 0, pairs, lanes)
    first_one[3 * RIM] = mark
    first_two[3 * RIM] = mark
    for last, first, chosen in (
        (first_one, first_two, place.even),
        (first_two, first_one, jnp.logical_not(place.even)),
    ):

        @pl.when(chosen)
        def _():
            for part in range(3):
                last[part * RIM : (part + 1) * RIM] = own[part, rows - RIM : rows]
                first[part * RIM : (part + 1) * RIM] = own[part, 0:RIM]


def frame_kernel(tick, flow_in, features, frame, natural, scratch, sems, flow):
    _, pairs, lanes = frame.shape
    copies = [
        pltpu.make_async_copy(features.at[tick], natural, sems.at[0]),
        pltpu.make_async_copy(flow_in, flow, sems.at[1]),
    ]
    for copy in copies:
        copy.start()
    copies[0].wait()
    for r, row in enumerate(natural_to_rows(scratch, natural)):
        frame[1 + r] = row
    copies[1].wait()
    frame[0] = shift_row(flow, tick, pairs, lanes)


def own_terms(sources, w_ref, acc, ops, padded, low, sub):
    rows = ops.shape[1]
    at = 0
    for part, (row, shift, interleaved) in enumerate(sources):
        for r in range(rows):
            stage(padded, at, row(r), interleaved)
            if shift is None:
                put_plain(ops, (part, r), padded, at, low)
            else:
                put_warped(ops, (part, r), padded, at, shift, low, sub)
            at += 1
    first, end = local_span(rows)
    fetches = [lambda r, h, part=part: ops[part, r - RIM, h] for part in range(3)]
    acc[...] = two_row_conv(fetches, first, end - first, w_ref, (0, 1, 2))


def start_kernel(slots, index, clip, flow, own, w_ref, acc, ops, padded):
    lanes = own.shape[3]
    keep = Place(index, clip, slots).keep(0)
    clear_pads(padded)

    def kept(part):
        return lambda r: jnp.where(keep, own[part, r].astype(F32), 0.0)

    own_terms(
        (
            (kept(0), flow[0, 0, 0], False),
            (kept(1), flow[0, 1, 0], False),
            (lambda r: own[2, r].astype(F32), None, False),
        ),
        w_ref, acc, ops, padded, lane_low(lanes), sublane(lanes),
    )


def ahead_kernel(
    slots, tick, index, clip, latest, prev, feat, w_ref, acc, ops, natural, padded, plain_rows,
    *copying,
):
    rows, _, lanes = latest.shape
    place = Place(index, clip, slots)
    keep_latest = place.keep(tick)
    keep_earlier = keep_latest & place.keep(tick - 1)
    shift = scalars_of(feat[0])
    clear_pads(padded)
    for r in range(rows):
        plain_rows[r] = latest[r].astype(F32)
    own_terms(
        (
            (lambda r: jnp.where(keep_latest, plain_rows[r], 0.0), shift[0], True),
            (lambda r: jnp.where(keep_earlier, prev[r].astype(F32), 0.0), shift[1], tick > 1),
            (lambda r: feat[1 + r].astype(F32), None, False),
        ),
        w_ref, acc, ops, padded, lane_low(lanes), sublane(lanes),
    )
    if copying:
        natural_rows, sem = copying
        rows_to_natural(natural_rows, plain_rows)
        copy = pltpu.make_async_copy(natural_rows, natural.at[0], sem)
        copy.start()
        copy.wait()
    else:
        rows_to_natural(natural, plain_rows)


def rows_to_natural(natural, plain_rows):
    rows, pairs, lanes = plain_rows.shape
    groups = pairs // SUB
    flat = plain_rows.reshape(rows * pairs, lanes)
    for v in range(groups):
        for s in range(SUB):
            pair = groups * s + v
            tile = flat[pl.ds(SUB * v + s, rows, stride=pairs), :]
            natural[:, pair * lanes : (pair + 1) * lanes] = tile.astype(BF16)


def finish_kernel(
    slots, tick, index, clip, acc_in, ops, halo_one, halo_two, prev, w_ref,
    latest, natural, sends, window, layers, padded, plain_rows,
):
    _, rows, _, pairs, lanes = ops.shape
    place = Place(index, clip, slots)
    even = place.even
    low, sub = lane_low(lanes), sublane(lanes)
    keep = place.keep(tick)
    keep_both = keep if tick == 0 else keep & place.keep(tick - 1)

    def above(r, one=halo_one, two=halo_two):
        return jnp.where(even, two[r], one[r])

    def below(r, one=halo_one, two=halo_two):
        return jnp.where(even, one[r], two[r])

    if tick == 0:
        marks = 3 * RIM
        sides = [
            (side, [lambda r, k=k, side=side: side(k * RIM + r) for k in range(3)],
             scalars_of(side(marks)))
            for side in (above, below)
        ]
    else:
        sides = [
            (
                side,
                [
                    lambda r, side=side: side(r),
                    lambda r, side=side: side(r, *prev),
                    lambda r, side=side: side(RIM + 1 + r),
                ],
                scalars_of(side(RIM)),
            )
            for side in (above, below)
        ]

    def operand(part):
        def fetch(r, h):
            if r < RIM:
                return window[part, r, h]
            if r < RIM + rows:
                return ops[part, r - RIM, h]
            return window[part, r - rows, h]

        return fetch

    count = (rows + 2 * RIM - 2) // 2
    first, end = local_span(rows)
    split = end + 1
    clear_pads(padded)
    at = 0
    terms = {}
    for part in (2, 1, 0):
        for which, (side, sources, shift) in enumerate(sides):
            ok = place.above if which == 0 else place.below
            if part < 2:
                ok = ok & (keep, keep_both)[part]
            for r in range(RIM):
                row = sources[part](r).astype(F32)
                stage(padded, at, jnp.where(ok, row, 0.0), tick > part and part < 2)
                slot = which * RIM + r
                if part < 2:
                    put_warped(window, (part, slot), padded, at, shift[part], low, sub)
                else:
                    put_plain(window, (part, slot), padded, at, low)
                at += 1
            begin, stop = ((0, first), (end, count))[which]
            term = two_row_conv([operand(part)], begin, stop - begin, w_ref, (part,))
            terms[begin] = terms[begin] + term if begin in terms else term


    def emit(layer, pair, both):
        margin = RIM - 1 - layer
        for q in range(2):
            r = 2 * pair + q
            value = both[:, q * lanes : (q + 1) * lanes]
            if layer == 0:
                value = jnp.maximum(value, 0.1 * value)
            elif layer % 2 == 1:
                value = jnp.maximum(value, 0.0)
            else:
                value = value + layers[layer - 2][r + 2, 0].astype(F32)
            if r < margin:
                value = jnp.where(place.above, value, 0.0)
            elif r >= margin + rows:
                value = jnp.where(place.below, value, 0.0)
            if layer < 2 * RES_BLOCKS:
                put(layers[layer], (r,), value, low, sub)
            else:
                if sends:
                    latest[r] = value.astype(BF16)
                else:
                    plain_rows[r] = value

    for begin, stop in ((0, first), (first, end), (end, count)):
        for k in range(begin, stop):
            source = acc_in if begin == first else terms[begin]
            emit(0, k, source[(k - begin) * pairs : (k - begin + 1) * pairs])
    for layer in range(1, 2 * RES_BLOCKS + 1):
        count -= 1
        split -= 1
        for begin, stop in ((0, split), (split, count)):
            made = two_row_conv(
                [lambda r, h: layers[layer - 1][r, h]], begin, stop - begin, w_ref, (2 + layer,)
            )
            for k in range(begin, stop):
                emit(layer, k, made[(k - begin) * pairs : (k - begin + 1) * pairs])
    if not sends:
        rows_to_natural(natural, plain_rows)
        return
    send_one, send_two = sends

    @pl.when(even)
    def _():
        send_one[...] = latest[rows - RIM : rows]
        send_two[...] = latest[0:RIM]

    @pl.when(jnp.logical_not(even))
    def _():
        send_one[...] = latest[0:RIM]
        send_two[...] = latest[rows - RIM : rows]


def weight_kernel(join, res, w_ref):
    channels = join.shape[1]
    zero = jnp.zeros((channels, channels), F32)

    def fill(layer, a, taps):
        before, here, after = taps
        left = jnp.concatenate([here, after, zero, before], axis=1)
        right = jnp.concatenate([before, here, after, zero], axis=1)
        w_ref[layer, a] = jnp.concatenate([left, right], axis=0).T.astype(BF16)

    for a in range(3):
        whole = join[a].astype(F32)
        for part in range(3):
            starts = [(3 * b + part) * channels for b in range(3)]
            fill(part, a, [whole[:, at : at + channels] for at in starts])
    for layer in range(res.shape[0]):
        for a in range(3):
            whole = res[layer, a].astype(F32)
            fill(3 + layer, a, [whole[:, b * channels : (b + 1) * channels] for b in range(3)])


def shards(features, carried, flow_shift, clip_start, join_weight, res_weight):
    rows = features.shape[1]
    wide = features.shape[2]
    channels = join_weight.shape[2]
    lanes = 2 * channels
    pairs = wide // lanes
    slots = lax.axis_size("rows")
    bands = slots // SECTIONS
    lead = bands // 2
    index = lax.axis_index("rows")
    even = (index + (slots - lead)) % 2 == 0
    index = index.astype(jnp.int32).reshape(1)

    def route(move):
        return [(i, move(i) % slots) for i in range(slots)]

    def is_even(i):
        return (i - lead) % 2 == 0

    swap_one = route(lambda i: i + 1 if is_even(i) else i - 1)
    swap_two = route(lambda i: i - 1 if is_even(i) else i + 1)

    def shift_by(count):
        return route(lambda i: i + count)

    def send(block, path):
        return lax.ppermute(block, "rows", path)

    flow = jnp.transpose(flow_shift, (1, 2, 0))
    made = rows + 2 * (RIM - 1)
    long = pairs + 2 * PAD
    first, end = local_span(rows)
    params = pltpu.CompilerParams(vmem_limit_bytes=GRANT)

    def cost(pairs_done, depth):
        return pl.CostEstimate(
            flops=pairs_done * pairs * depth * 16 * lanes * lanes,
            bytes_accessed=4 << 20,
            transcendentals=0,
        )

    def operands(*lead_shape):
        return lead_shape + (2, pairs, lanes)

    def pack():
        def kernel(*refs):
            pack_kernel(slots, *refs)

        halo = jax.ShapeDtypeStruct((3 * RIM + 1, pairs, lanes), BF16)
        return pl.pallas_call(
            kernel,
            out_shape=(jax.ShapeDtypeStruct((3, rows, pairs, lanes), BF16), halo, halo),
            in_specs=[SMEM, HBM, HBM, HBM],
            out_specs=(VMEM, VMEM, VMEM),
            scratch_shapes=[
                pltpu.VMEM((3, rows, wide), BF16),
                pltpu.VMEM((3, rows * (pairs + SUB), lanes), F32),
                pltpu.SemaphoreType.DMA((4,)),
                pltpu.SMEM(flow.shape, jnp.int32),
            ],
            compiler_params=params,
            name="pack",
        )(index, in_hbm(flow), in_hbm(carried), in_hbm(features))

    def framed(tick, features):
        def kernel(*refs):
            frame_kernel(tick, *refs)

        return pl.pallas_call(
            kernel,
            out_shape=jax.ShapeDtypeStruct((rows + 1, pairs, lanes), BF16),
            in_specs=[HBM, HBM],
            out_specs=VMEM,
            scratch_shapes=[
                pltpu.VMEM((rows, wide), BF16),
                pltpu.VMEM((rows * (pairs + SUB), lanes), F32),
                pltpu.SemaphoreType.DMA((2,)),
                pltpu.SMEM(flow.shape, jnp.int32),
            ],
            compiler_params=params,
        )(in_hbm(flow), in_hbm(features))

    def start(own):
        def kernel(*refs):
            start_kernel(slots, *refs)

        return pl.pallas_call(
            kernel,
            out_shape=(
                jax.ShapeDtypeStruct(((end - first) * pairs, 2 * lanes), F32),
                jax.ShapeDtypeStruct(operands(3, rows), BF16),
            ),
            in_specs=[SMEM, SMEM, SMEM, VMEM, VMEM],
            out_specs=(VMEM, VMEM),
            scratch_shapes=[pltpu.VMEM((3 * rows, long, lanes), F32)],
            compiler_params=params,
            cost_estimate=cost(end - first, 3),
            name="start",
        )(index, clip_start, flow, own, weights)

    def ahead(tick, latest, prev, feat):
        def kernel(*refs):
            ahead_kernel(slots, tick, *refs)

        whole = (TICKS,) if tick == 1 else ()
        return pl.pallas_call(
            kernel,
            out_shape=(
                jax.ShapeDtypeStruct(((end - first) * pairs, 2 * lanes), F32),
                jax.ShapeDtypeStruct(operands(3, rows), BF16),
                jax.ShapeDtypeStruct(whole + (rows, wide), BF16),
            ),
            in_specs=[SMEM, SMEM] + [VMEM] * 4,
            out_specs=(VMEM, VMEM, HBM if whole else VMEM),
            scratch_shapes=[
                pltpu.VMEM((3 * rows, long, lanes), F32),
                pltpu.VMEM((rows, pairs, lanes), F32),
            ]
            + ([pltpu.VMEM((rows, wide), BF16), pltpu.SemaphoreType.DMA] if whole else []),
            compiler_params=params,
            cost_estimate=cost(end - first, 3),
        )(index, clip_start, latest, prev, feat, weights)

    def finish(tick, acc, ops, one, two, prev=()):
        last = tick + 1 == TICKS
        parts = ops.shape[0]

        def kernel(index, clip, acc_in, ops, one, two, *rest):
            before, (w_ref, *rest) = rest[: len(prev)], rest[len(prev) :]
            if last:
                natural, *scratch = rest
                latest, sends = None, ()
            else:
                latest, send_one, send_two, *scratch = rest
                natural, sends = None, (send_one, send_two)
            window, *layers, padded, plain_rows = scratch
            finish_kernel(
                slots, tick, index, clip, acc_in, ops, one, two, before, w_ref,
                latest, natural, sends, window, layers, padded, plain_rows,
            )

        halo = jax.ShapeDtypeStruct((RIM, pairs, lanes), BF16)
        if last:
            outs = (jax.ShapeDtypeStruct((rows, wide), BF16),)
        else:
            outs = (jax.ShapeDtypeStruct((rows, pairs, lanes), BF16), halo, halo)
        return pl.pallas_call(
            kernel,
            out_shape=outs,
            in_specs=[SMEM, SMEM] + [VMEM] * (5 + len(prev)),
            out_specs=(VMEM,) * len(outs),
            scratch_shapes=[pltpu.VMEM(operands(parts, 2 * RIM), BF16)]
            + [pltpu.VMEM(operands(made - 2 * layer), BF16) for layer in range(2 * RES_BLOCKS)]
            + [
                pltpu.VMEM((parts * 2 * RIM, long, lanes), F32),
                pltpu.VMEM((rows, pairs, lanes), F32),
            ],
            compiler_params=params,
            cost_estimate=cost(made + made // 2 * parts, 1),
        )(index, clip_start, acc, ops, one, two, *prev, weights)

    own, first_one, first_two = pack()
    later_features, first_one, first_two = lax.optimization_barrier(
        (features, first_one, first_two)
    )
    halo_two = send(first_two, swap_two)
    halo_one = send(first_one, swap_one)
    frame = framed(1, later_features)
    frame, own, join_weight, res_weight = lax.optimization_barrier(
        (frame, own, join_weight, res_weight)
    )

    def bring(tick, frame):
        return send(frame, shift_by(-bands * tick))

    feat = bring(1, frame)
    weights = pl.pallas_call(
        weight_kernel,
        out_shape=jax.ShapeDtypeStruct((3 + 2 * RES_BLOCKS, 3, 2 * lanes, lanes), BF16),
        in_specs=[VMEM, VMEM],
        out_specs=VMEM,
        compiler_params=params,
        name="weights",
    )(jnp.transpose(join_weight, (0, 2, 1)), jnp.transpose(res_weight, (0, 1, 3, 2)))
    acc, ops = start(own)
    begin_one = jnp.where(even, rows + 1 - RIM, 1)
    begin_two = jnp.where(even, 1, rows + 1 - RIM)

    def with_rim(block, frame, begin):
        rim = lax.dynamic_slice_in_dim(frame, begin, RIM, axis=0)
        return jnp.concatenate([block, frame[0:1], rim], axis=0)

    last_features = later_features
    second_feat = bring(2, framed(2, last_features))
    one, two = halo_one, halo_two
    prev = own[0]
    outs = finish(0, acc, ops, one, two)
    for tick in range(1, TICKS):
        latest, send_one, send_two = outs
        feat, latest, send_one, send_two = lax.optimization_barrier(
            (feat, latest, send_one, send_two)
        )
        before = one, two
        two = send(with_rim(send_two, feat, begin_two), swap_two)
        one = send(with_rim(send_one, feat, begin_one), swap_one)
        acc, ops, natural = ahead(tick, latest, prev, feat)
        if tick == 1:
            result = natural
        else:
            moved = send(natural, shift_by(bands * (tick - 1)))
            result = lax.dynamic_update_slice_in_dim(result, moved[None], tick - 1, 0)
        prev = latest
        feat = second_feat
        outs = finish(tick, acc, ops, one, two, before)
    moved = send(outs[0], shift_by(bands * (TICKS - 1)))
    return lax.dynamic_update_slice_in_dim(result, moved[None], TICKS - 1, 0)


def solution(mesh):
    in_specs = (
        P(None, ("groups", "rows"), None),
        P(None, ("groups", "rows"), None),
        P(None, ("groups", "rows"), None),
        P("groups"),
        P(),
        P(),
    )
    out_specs = P(None, ("groups", "rows"), None)

    return jax.shard_map(
        shards, mesh=mesh, in_specs=in_specs, out_specs=out_specs, check_vma=False
    )
```
